512 devices in a mesh: wide: 64 (over z, y), rows: 8 (over x, core).
Axes of the slice: x: 4, y: 8, z: 8, core: 2. Of those that a mesh axis runs over, the one named last changes fastest.
Arguments:
- slabs: bfloat16 [64, 8, 10, 32, 128], P('wide', 'rows'), may hold values from -6 to 6
- dest: int32 [64, 8, 10], P('wide', 'rows'), may hold values from 0 to 63, as said below
- pos: int32 [64, 8, 10], P('wide', 'rows'), may hold values from 0 to 9, as said below
- lengths: int32 [64], P('wide'), may hold values from 1 to 5
- cot: bfloat16 [64, 5, 16, 32, 128], P('wide', None, 'rows'), may hold values from -6 to 6
- w_first: bfloat16 [3456, 128], P('wide'), may hold values from -0.109375 to 0.109375
- w_second: bfloat16 [3456, 128], P('wide'), may hold values from -0.109375 to 0.109375
Outputs:
- block_out: bfloat16 [64, 5, 16, 32, 128], P('wide', None, 'rows')
- grad_input: bfloat16 [64, 5, 16, 32, 128], P('wide', None, 'rows')
- grad_w_first: float32 [3456, 128], P('wide')
- grad_w_second: float32 [3456, 128], P('wide')
The draws below stay inside these ranges and needn't reach their ends.
Inputs may be any that keep to these rules, and one draw needn't show every extreme that they name: `dest`: within a band no loader sends more than one slab to any clip; every clip receives exactly 10 slabs in each band. `pos`: for every clip and band the 10 slabs it receives carry the places 0 to 9, each once.
All inputs are finite; a program needn't handle non-finite values.
Results may differ from the reference program's by a relative error of at most 0.018.
Values may be sent and summed in bfloat16 or wider, within the bound.
A program may use at most 64 MiB of HBM per device.

```python
import math
import jax
import jax.numpy as jnp
from jax import lax

C = 128
TAPS = 27
FRAMES = 5
ROWS_DEV = 2
COLS = 32
CLIPS = 64
LOADERS = 64
SLABS = 10
CAP = 1
TILE_ROWS = 16
ALL_CELLS = 163840
N_ROWS = 8


def packing_lists(key):
    shift_keys = jax.random.split(jax.random.fold_in(key, 17), N_ROWS)
    order_keys = jax.random.split(jax.random.fold_in(key, 23), N_ROWS)
    source_pool = jnp.arange(LOADERS * CAP, dtype=jnp.int32) % LOADERS
    needed = jnp.array([1, LOADERS // 2, LOADERS - 1], dtype=jnp.int32)
    half_point = LOADERS // 2
    remaining = jnp.concatenate([source_pool[0:1], source_pool[2:half_point], source_pool[half_point + 1:LOADERS - 1], source_pool[LOADERS:]])

    def pick_shifts(one_key, other_key):
        chosen = jnp.concatenate([needed, jax.random.permutation(one_key, remaining)])[:SLABS]
        return jax.random.permutation(other_key, chosen)
    shifts = jax.vmap(pick_shifts)(shift_keys, order_keys)
    loader_ids = jnp.arange(LOADERS, dtype=jnp.int32)
    destination = (loader_ids[:, None, None] + shifts[None, :, :]) % LOADERS
    place_keys = jax.random.split(jax.random.fold_in(key, 29), N_ROWS * LOADERS)

    def pick_places(one_key):
        return jax.random.permutation(one_key, SLABS).astype(jnp.int32)
    orders = jax.vmap(pick_places)(place_keys).reshape(N_ROWS, LOADERS, SLABS)
    band_ids = jnp.arange(N_ROWS, dtype=jnp.int32)[None, :, None]
    slab_ids = jnp.arange(SLABS, dtype=jnp.int32)[None, None, :]
    places = orders[band_ids, destination, slab_ids]
    return (destination.astype(jnp.int32), places.astype(jnp.int32))


def draw_dest(key, part):
    return packing_lists(key)[0]


def draw_pos(key, part):
    return packing_lists(key)[1]


def place_ends(drawn, key, low, top_value):
    spot = [jax.random.randint(jax.random.fold_in(key, axis), (), 0, length) for axis, length in enumerate(drawn.shape)]
    longest = drawn.shape.index(max(drawn.shape))
    neighbour = spot[:longest] + [(spot[longest] + 1) % drawn.shape[longest]] + spot[longest + 1:]
    return drawn.at[tuple(spot)].set(low).at[tuple(neighbour)].set(top_value)


def steps_of(key, dims, pieces, low, high):
    level = 1.0
    for dim, shards_of in pieces:
        heights = jax.random.uniform(jax.random.fold_in(jax.random.fold_in(key, 6), dim), (shards_of,), jnp.float32, low / len(pieces), high / len(pieces))
        level = level * jnp.repeat(jnp.exp(heights), dims[dim] // shards_of).reshape((-1,) + (1,) * (len(dims) - 1 - dim))
    return level


def normal_values(rng, dims, width, most, cuts=(), held_as=jnp.bfloat16):
    entries = jax.random.normal(rng, dims, jnp.float32) * width
    if len(cuts) > 0:
        entries = steps_of(rng, dims, cuts, -0.22, 0.18) * entries
    return jnp.clip(entries, min=-most, max=most).astype(held_as)


def setup_inputs(seed: int = 0) -> dict:
    splits = jax.random.split(jax.random.key(seed), 8)
    slabs = normal_values(splits[0], (LOADERS, N_ROWS, SLABS, COLS, C), 1.0, 6.0, ((0, 64), (1, 8)))
    dest = draw_dest(jax.random.fold_in(splits[7], 71), 0)
    pos = draw_pos(jax.random.fold_in(splits[7], 71), 0)
    lengths = place_ends(jax.random.randint(splits[3], (CLIPS,), 1, FRAMES + 1), jax.random.fold_in(splits[3], 1), 1, FRAMES).astype(jnp.int32)
    cot = normal_values(splits[4], (CLIPS, FRAMES, TILE_ROWS, COLS, C), 1.0, 6.0, ((0, 64), (2, 8)))
    w_first = normal_values(splits[5], (TAPS * C, C), (TAPS * C) ** -0.5, 0.109375, ((0, 64),))
    w_second = normal_values(splits[6], (TAPS * C, C), (TAPS * C) ** -0.5, 0.109375, ((0, 64),))
    return dict(slabs=slabs, dest=dest, pos=pos, lengths=lengths, cot=cot, w_first=w_first, w_second=w_second)


def silu_slope(values):
    sig = jax.nn.sigmoid(values)
    return sig * (1.0 + values * (1.0 - sig))

def causal_conv(field, kernel):
    padded = jnp.concatenate([field[:1], field[:1], field], axis=0)
    result = lax.conv_general_dilated(padded[None], kernel, (1, 1, 1), ((0, 0), (1, 1), (1, 1)), dimension_numbers=('NDHWC', 'DHWIO', 'NDHWC'), precision=lax.Precision.HIGHEST, preferred_element_type=jnp.float32)
    return result[0]

def to_bf16(values):
    rounded = values.astype(jnp.bfloat16)
    return lax.optimization_barrier(rounded).astype(jnp.float32)

def reference(slabs, dest, pos, lengths, cot, w_first, w_second):
    band_ids = jnp.arange(N_ROWS, dtype=jnp.int32)[None, :, None]
    targets = (band_ids * (CLIPS * SLABS) + dest.astype(jnp.int32) * SLABS + pos.astype(jnp.int32)).astype(jnp.int32)
    placed = jnp.zeros((N_ROWS * CLIPS * SLABS, COLS, C), jnp.bfloat16)
    placed = placed.at[targets.reshape(-1)].set(slabs.reshape(-1, COLS, C))
    placed = placed.reshape(N_ROWS, CLIPS, FRAMES, ROWS_DEV, COLS, C)
    tiles = jnp.transpose(placed, (1, 2, 0, 3, 4, 5)).reshape(CLIPS, FRAMES, TILE_ROWS, COLS, C)
    kernel_first = w_first.astype(jnp.float32).reshape(3, 3, 3, C, C)
    kernel_second = w_second.astype(jnp.float32).reshape(3, 3, 3, C, C)
    frame_ids = jnp.arange(FRAMES, dtype=jnp.int32)

    def per_clip(totals, inputs):
        tile, upstream, length = inputs
        tile_wide = tile.astype(jnp.float32)
        first = to_bf16(jax.nn.silu(tile_wide))
        act = to_bf16(causal_conv(first, kernel_first))
        second = to_bf16(jax.nn.silu(act))
        block_out = (tile_wide + causal_conv(second, kernel_second)).astype(jnp.bfloat16)
        live = (frame_ids < length)[:, None, None, None]
        out_grad = jnp.where(live, upstream.astype(jnp.float32), 0.0)
        pull_second = jax.vjp(causal_conv, second, kernel_second)[1]
        hidden_grad, weight_second = pull_second(out_grad)
        act_grad = to_bf16(hidden_grad * silu_slope(act))
        pull_first = jax.vjp(causal_conv, first, kernel_first)[1]
        first_grad, weight_first = pull_first(act_grad)
        grad_input = (out_grad + first_grad * silu_slope(tile_wide)).astype(jnp.bfloat16)
        return ((totals[0] + weight_first, totals[1] + weight_second), (block_out, grad_input))
    zeros = jnp.zeros((3, 3, 3, C, C), jnp.float32)
    totals, outputs = lax.scan(per_clip, (zeros, zeros), (tiles, cot, lengths))
    scale = 1.0 / math.sqrt(ALL_CELLS)
    grad_w_first = (totals[0] * scale).reshape(TAPS * C, C)
    grad_w_second = (totals[1] * scale).reshape(TAPS * C, C)
    return (outputs[0], outputs[1], grad_w_first, grad_w_second)
```

```python
import math

import jax
import jax.numpy as jnp
from jax import lax
from jax.sharding import PartitionSpec as P


def with_halo(block, sides, width):
    for axis, dim in sides:
        count = lax.axis_size(axis)
        forward = [(i, i + 1) for i in range(count - 1)]
        backward = [(target, source) for source, target in forward]
        low = lax.ppermute(
            lax.slice_in_dim(block, block.shape[dim] - width, None, axis=dim), axis, forward
        )
        high = lax.ppermute(lax.slice_in_dim(block, 0, width, axis=dim), axis, backward)
        block = jnp.concatenate([low, block, high], axis=dim)
    return block


def silu_slope(values):
    sig = jax.nn.sigmoid(values)
    return sig * (1.0 + values * (1.0 - sig))


def conv_forward(extended, kernel):
    padded = jnp.concatenate([extended[:1], extended[:1], extended], axis=0)
    result = lax.conv_general_dilated(
        padded[None],
        kernel,
        (1, 1, 1),
        ((0, 0), (0, 0), (1, 1)),
        dimension_numbers=("NDHWC", "DHWIO", "NDHWC"),
        preferred_element_type=jnp.float32,
    )
    return result[0]


def conv_weight_grad(extended, upstream):
    padded = jnp.concatenate([extended[:1], extended[:1], extended], axis=0)
    result = lax.conv_general_dilated(
        padded[None],
        upstream[None],
        (1, 1, 1),
        ((0, 0), (0, 0), (1, 1)),
        dimension_numbers=("CDHWN", "IDHWO", "NDHWC"),
        preferred_element_type=jnp.float32,
    )
    channels = extended.shape[-1]
    return jnp.transpose(result, (1, 2, 3, 0, 4)).reshape(27 * channels, upstream.shape[-1])


def conv_data_grad(upstream_ext, kernel):
    padded = jnp.pad(upstream_ext, ((2, 2), (0, 0), (0, 0), (0, 0)))
    flipped = kernel[::-1, ::-1, ::-1]
    result = lax.conv_general_dilated(
        padded[None],
        flipped,
        (1, 1, 1),
        ((0, 0), (0, 0), (1, 1)),
        dimension_numbers=("NDHWC", "DHWOI", "NDHWC"),
        preferred_element_type=jnp.float32,
    )[0]
    head = (result[0] + result[1] + result[2])[None]
    return jnp.concatenate([head, result[3:]], axis=0)


def gather_weights(w_first, w_second, band_count):
    rows_local, channels = w_first.shape
    part = channels // band_count
    me = lax.axis_index("rows")
    both = jnp.stack([w_first, w_second]).reshape(2, rows_local, band_count, part)
    mine = lax.dynamic_index_in_dim(both, me, axis=2, keepdims=False)
    mine = mine.reshape(1, 2, rows_local * part)
    wide_all = lax.all_gather(mine, "wide", axis=0, tiled=True)
    full = lax.all_gather(wide_all[None], "rows", axis=0, tiled=True)
    count = wide_all.shape[0]
    full = full.reshape(band_count, count, 2, rows_local, part)
    full = jnp.transpose(full, (2, 1, 3, 0, 4)).reshape(2, count * rows_local, channels)
    shape = (3, 3, 3, channels, channels)
    return full[0].reshape(shape), full[1].reshape(shape)


def reduce_weight_grads(weight_first, weight_second, band_count, wide_size):
    total_rows, channels = weight_first.shape
    part = channels // band_count
    chunk = total_rows // wide_size
    both = jnp.stack([weight_first, weight_second]).astype(jnp.bfloat16)
    both = both.reshape(2, total_rows, band_count, part)
    both = jnp.transpose(both, (2, 0, 1, 3)).reshape(band_count, 2, total_rows * part)
    band_sum = lax.psum_scatter(both, "rows", scatter_dimension=0, tiled=True)
    band_sum = band_sum.astype(jnp.float32).reshape(2, wide_size, chunk * part)
    band_sum = jnp.transpose(band_sum, (1, 0, 2))
    share = lax.psum_scatter(band_sum, "wide", scatter_dimension=0, tiled=True)
    joined = lax.all_gather(share, "rows", axis=0, tiled=True)
    joined = joined.reshape(band_count, 2, chunk, part)
    joined = jnp.transpose(joined, (1, 2, 0, 3)).reshape(2, chunk, channels)
    return joined[0], joined[1]


def body(slabs, dest, pos, lengths, cot, w_first, w_second):
    wide_size = lax.axis_size("wide")
    band_count = lax.axis_size("rows")
    slab_count = slabs.shape[2]
    columns = slabs.shape[3]
    channels = slabs.shape[4]
    frames = cot.shape[1]
    band_rows = cot.shape[2]
    capacity = -(-slab_count // wide_size)
    slot_count = wide_size * capacity
    targets = dest[0, 0]
    places = pos[0, 0]
    ranking = jnp.arange(slab_count, dtype=jnp.int32)
    earlier = (targets[None, :] == targets[:, None]) & (ranking[None, :] < ranking[:, None])
    slab_rank = jnp.sum(earlier.astype(jnp.int32), axis=1)
    slot_of = targets * capacity + slab_rank
    placing = slot_of[None, :] == jnp.arange(slot_count, dtype=jnp.int32)[:, None]
    flat_slabs = slabs[0, 0].reshape(slab_count, columns * channels)
    outgoing = jnp.dot(placing.astype(jnp.bfloat16), flat_slabs, preferred_element_type=jnp.float32)
    outgoing = outgoing.astype(jnp.bfloat16).reshape(wide_size, capacity, columns * channels)
    labels = jnp.sum(jnp.where(placing, places[None, :] + 1, 0), axis=1) - 1
    labels = labels.reshape(wide_size, capacity)
    arrived, arrived_places = (
        lax.all_to_all(outgoing, "wide", split_axis=0, concat_axis=0, tiled=True),
        lax.all_to_all(labels, "wide", split_axis=0, concat_axis=0, tiled=True),
    )
    settle = (
        arrived_places.reshape(slot_count)[None, :]
        == jnp.arange(slab_count, dtype=jnp.int32)[:, None]
    )
    tile = jnp.dot(
        settle.astype(jnp.bfloat16),
        arrived.reshape(slot_count, columns * channels),
        preferred_element_type=jnp.float32,
    )
    tile = tile.astype(jnp.bfloat16).reshape(frames, band_rows, columns, channels)
    kernel_first, kernel_second = gather_weights(w_first, w_second, band_count)
    tile_wide = tile.astype(jnp.float32)
    first = jax.nn.silu(tile_wide).astype(jnp.bfloat16)
    first_ext = with_halo(first, (("rows", 1),), 1)
    act = conv_forward(first_ext, kernel_first).astype(jnp.bfloat16)
    second = jax.nn.silu(act.astype(jnp.float32)).astype(jnp.bfloat16)
    second_ext = with_halo(second, (("rows", 1),), 1)
    block_out = (tile_wide + conv_forward(second_ext, kernel_second)).astype(jnp.bfloat16)
    live = (jnp.arange(frames, dtype=jnp.int32) < lengths[0])[:, None, None, None]
    out_grad = jnp.where(live, cot[0], jnp.zeros_like(cot[0]))
    out_grad_ext = with_halo(out_grad, (("rows", 1),), 1)
    weight_second = conv_weight_grad(second_ext, out_grad)
    hidden_grad = conv_data_grad(out_grad_ext, kernel_second)
    act_grad = (hidden_grad * silu_slope(act.astype(jnp.float32))).astype(jnp.bfloat16)
    act_grad_ext = with_halo(act_grad, (("rows", 1),), 1)
    weight_first = conv_weight_grad(first_ext, act_grad)
    first_grad = conv_data_grad(act_grad_ext, kernel_first)
    grad_input = (out_grad.astype(jnp.float32) + first_grad * silu_slope(tile_wide)).astype(
        jnp.bfloat16
    )
    scale = 1.0 / math.sqrt(frames * band_rows * columns * band_count * wide_size)
    weight_first = weight_first * scale
    weight_second = weight_second * scale
    share_first, share_second = reduce_weight_grads(weight_first, weight_second, band_count, wide_size)
    return (block_out[None], grad_input[None], share_first, share_second)


def solution(mesh):
    return jax.shard_map(
        body,
        mesh=mesh,
        in_specs=(
            P("wide", "rows", None, None, None),
            P("wide", "rows", None),
            P("wide", "rows", None),
            P("wide"),
            P("wide", None, "rows", None, None),
            P("wide", None),
            P("wide", None),
        ),
        out_specs=(
            P("wide", None, "rows", None, None),
            P("wide", None, "rows", None, None),
            P("wide", None),
            P("wide", None),
        ),
        check_vma=False,
    )
```

```python
import math

import jax
import jax.numpy as jnp
from jax import lax
from jax.sharding import PartitionSpec as P


def with_halo(block, sides, width):
    for axis, dim in sides:
        count = lax.axis_size(axis)
        forward = [(i, i + 1) for i in range(count - 1)]
        backward = [(target, source) for source, target in forward]
        low = lax.ppermute(
            lax.slice_in_dim(block, block.shape[dim] - width, None, axis=dim), axis, forward
        )
        high = lax.ppermute(lax.slice_in_dim(block, 0, width, axis=dim), axis, backward)
        block = jnp.concatenate([low, block, high], axis=dim)
    return block


def silu_slope(values):
    sig = jax.nn.sigmoid(values)
    return sig * (1.0 + values * (1.0 - sig))


def conv_forward(extended, kernel):
    padded = jnp.concatenate([extended[:1], extended[:1], extended], axis=0)
    result = lax.conv_general_dilated(
        padded[None],
        kernel,
        (1, 1, 1),
        ((0, 0), (0, 0), (1, 1)),
        dimension_numbers=("NDHWC", "DHWIO", "NDHWC"),
        preferred_element_type=jnp.float32,
    )
    return result[0]


def conv_weight_grad(extended, upstream):
    padded = jnp.concatenate([extended[:1], extended[:1], extended], axis=0)
    result = lax.conv_general_dilated(
        padded[None],
        upstream[None],
        (1, 1, 1),
        ((0, 0), (0, 0), (1, 1)),
        dimension_numbers=("CDHWN", "IDHWO", "NDHWC"),
        preferred_element_type=jnp.float32,
    )
    channels = extended.shape[-1]
    return jnp.transpose(result, (1, 2, 3, 0, 4)).reshape(27 * channels, upstream.shape[-1])


def conv_data_grad(upstream_ext, kernel):
    padded = jnp.pad(upstream_ext, ((2, 2), (0, 0), (0, 0), (0, 0)))
    flipped = kernel[::-1, ::-1, ::-1]
    result = lax.conv_general_dilated(
        padded[None],
        flipped,
        (1, 1, 1),
        ((0, 0), (0, 0), (1, 1)),
        dimension_numbers=("NDHWC", "DHWOI", "NDHWC"),
        preferred_element_type=jnp.float32,
    )[0]
    head = (result[0] + result[1] + result[2])[None]
    return jnp.concatenate([head, result[3:]], axis=0)


def gather_weights(w_first, w_second, band_count):
    rows_local, channels = w_first.shape
    part = channels // band_count
    me = lax.axis_index("rows")
    both = jnp.stack([w_first, w_second]).reshape(2, rows_local, band_count, part)
    mine = lax.dynamic_index_in_dim(both, me, axis=2, keepdims=False)
    mine = mine.reshape(1, 2, rows_local * part)
    count = lax.axis_size("wide")
    wide_all = lax.all_to_all(
        jnp.broadcast_to(mine, (count,) + mine.shape[1:]), "wide", 0, 0, tiled=True
    )
    full = lax.all_gather(wide_all[None], "rows", axis=0, tiled=True)
    full = full.reshape(band_count, count, 2, rows_local, part)
    full = jnp.transpose(full, (2, 1, 3, 0, 4)).reshape(2, count * rows_local, channels)
    shape = (3, 3, 3, channels, channels)
    return full[0].reshape(shape), full[1].reshape(shape)


def reduce_weight_grads(weight_first, weight_second, band_count, wide_size):
    total_rows, channels = weight_first.shape
    part = channels // band_count
    chunk = total_rows // wide_size
    both = jnp.stack([weight_first, weight_second]).astype(jnp.bfloat16)
    both = both.reshape(2, total_rows, band_count, part)
    both = jnp.transpose(both, (2, 0, 1, 3)).reshape(band_count, 2, total_rows * part)
    band_parts = lax.all_to_all(both, "rows", 0, 0, tiled=True)
    band_sum = jnp.sum(band_parts.astype(jnp.float32), axis=0)
    band_sum = jnp.transpose(band_sum.reshape(2, wide_size, chunk * part), (1, 0, 2))
    wide_parts = lax.all_to_all(band_sum, "wide", 0, 0, tiled=True)
    share = jnp.sum(wide_parts, axis=0, keepdims=True)
    joined = lax.all_to_all(
        jnp.broadcast_to(share, (band_count,) + share.shape[1:]), "rows", 0, 0, tiled=True
    )
    joined = joined.reshape(band_count, 2, chunk, part)
    joined = jnp.transpose(joined, (1, 2, 0, 3)).reshape(2, chunk, channels)
    return joined[0], joined[1]


def body(slabs, dest, pos, lengths, cot, w_first, w_second):
    wide_size = lax.axis_size("wide")
    band_count = lax.axis_size("rows")
    slab_count = slabs.shape[2]
    columns = slabs.shape[3]
    channels = slabs.shape[4]
    frames = cot.shape[1]
    band_rows = cot.shape[2]
    capacity = -(-slab_count // wide_size)
    slot_count = wide_size * capacity
    targets = dest[0, 0]
    places = pos[0, 0]
    ranking = jnp.arange(slab_count, dtype=jnp.int32)
    earlier = (targets[None, :] == targets[:, None]) & (ranking[None, :] < ranking[:, None])
    slab_rank = jnp.sum(earlier.astype(jnp.int32), axis=1)
    slot_of = targets * capacity + slab_rank
    placing = slot_of[None, :] == jnp.arange(slot_count, dtype=jnp.int32)[:, None]
    flat_slabs = slabs[0, 0].reshape(slab_count, columns * channels)
    outgoing = jnp.dot(placing.astype(jnp.bfloat16), flat_slabs, preferred_element_type=jnp.float32)
    outgoing = outgoing.astype(jnp.bfloat16).reshape(wide_size, capacity, columns * channels)
    labels = jnp.sum(jnp.where(placing, places[None, :] + 1, 0), axis=1) - 1
    labels = labels.reshape(wide_size, capacity)
    lane_block = 128
    tagged = jnp.concatenate(
        [outgoing, jnp.broadcast_to(labels.astype(jnp.bfloat16)[:, :, None], (wide_size, capacity, lane_block))],
        axis=2,
    )
    tagged = lax.all_to_all(tagged, "wide", split_axis=0, concat_axis=0, tiled=True)
    arrived = tagged[:, :, : columns * channels]
    arrived_places = tagged[:, :, columns * channels].astype(jnp.int32)
    settle = (
        arrived_places.reshape(slot_count)[None, :]
        == jnp.arange(slab_count, dtype=jnp.int32)[:, None]
    )
    tile = jnp.dot(
        settle.astype(jnp.bfloat16),
        arrived.reshape(slot_count, columns * channels),
        preferred_element_type=jnp.float32,
    )
    tile = tile.astype(jnp.bfloat16).reshape(frames, band_rows, columns, channels)
    kernel_first, kernel_second = gather_weights(w_first, w_second, band_count)
    tile_wide = tile.astype(jnp.float32)
    first = jax.nn.silu(tile_wide).astype(jnp.bfloat16)
    first_ext = with_halo(first, (("rows", 1),), 1)
    act = conv_forward(first_ext, kernel_first).astype(jnp.bfloat16)
    second = jax.nn.silu(act.astype(jnp.float32)).astype(jnp.bfloat16)
    second_ext = with_halo(second, (("rows", 1),), 1)
    block_out = (tile_wide + conv_forward(second_ext, kernel_second)).astype(jnp.bfloat16)
    live = (jnp.arange(frames, dtype=jnp.int32) < lengths[0])[:, None, None, None]
    out_grad = jnp.where(live, cot[0], jnp.zeros_like(cot[0]))
    out_grad_ext = with_halo(out_grad, (("rows", 1),), 1)
    weight_second = conv_weight_grad(second_ext, out_grad)
    hidden_grad = conv_data_grad(out_grad_ext, kernel_second)
    act_grad = (hidden_grad * silu_slope(act.astype(jnp.float32))).astype(jnp.bfloat16)
    act_grad_ext = with_halo(act_grad, (("rows", 1),), 1)
    weight_first = conv_weight_grad(first_ext, act_grad)
    first_grad = conv_data_grad(act_grad_ext, kernel_first)
    grad_input = (out_grad.astype(jnp.float32) + first_grad * silu_slope(tile_wide)).astype(
        jnp.bfloat16
    )
    scale = 1.0 / math.sqrt(frames * band_rows * columns * band_count * wide_size)
    weight_first = weight_first * scale
    weight_second = weight_second * scale
    share_first, share_second = reduce_weight_grads(weight_first, weight_second, band_count, wide_size)
    return (block_out[None], grad_input[None], share_first, share_second)


def solution(mesh):
    return jax.shard_map(
        body,
        mesh=mesh,
        in_specs=(
            P("wide", "rows", None, None, None),
            P("wide", "rows", None),
            P("wide", "rows", None),
            P("wide"),
            P("wide", None, "rows", None, None),
            P("wide", None),
            P("wide", None),
        ),
        out_specs=(
            P("wide", None, "rows", None, None),
            P("wide", None, "rows", None, None),
            P("wide", None),
            P("wide", None),
        ),
        check_vma=False,
    )
```

```python
import math

import jax
import jax.numpy as jnp
from jax import lax
from jax.sharding import PartitionSpec as P


def with_halo(block, sides, width):
    for axis, dim in sides:
        count = lax.axis_size(axis)
        forward = [(i, i + 1) for i in range(count - 1)]
        backward = [(target, source) for source, target in forward]
        low = lax.ppermute(
            lax.slice_in_dim(block, block.shape[dim] - width, None, axis=dim), axis, forward
        )
        high = lax.ppermute(lax.slice_in_dim(block, 0, width, axis=dim), axis, backward)
        block = jnp.concatenate([low, block, high], axis=dim)
    return block


def silu_slope(values):
    sig = jax.nn.sigmoid(values)
    return sig * (1.0 + values * (1.0 - sig))


def weight_pieces(w_first, w_second, band_count):
    rows_local, channels = w_first.shape
    part = channels // band_count
    me = lax.axis_index("rows")
    both = jnp.stack([w_first, w_second])
    mine = lax.dynamic_slice_in_dim(both, me * part, part, axis=2)
    return jnp.transpose(mine, (0, 2, 1)).reshape(2 * part * rows_local)


def assemble_weights(pieces, band_count, rows_local, channels):
    count = pieces.shape[0]
    part = channels // band_count
    block = pieces.reshape(count, 2, part, rows_local)
    block = jnp.transpose(block, (1, 2, 0, 3)).reshape(2, part, count * rows_local)
    full = lax.all_gather(block, "rows", axis=1, tiled=True)
    return full[0], full[1]


def reduce_weight_grads(grad_t, band_count, wide_size):
    _, channels, total_rows = grad_t.shape
    part = channels // band_count
    chunk = total_rows // wide_size
    blocks = grad_t.astype(jnp.bfloat16).reshape(2, band_count, part, total_rows)
    blocks = jnp.transpose(blocks, (1, 0, 2, 3))
    band_parts = lax.all_to_all(blocks, "rows", 0, 0, tiled=True)
    band_sum = jnp.sum(band_parts.astype(jnp.float32), axis=0)
    band_sum = band_sum.reshape(2, part, wide_size, chunk)
    band_sum = jnp.transpose(band_sum, (2, 0, 1, 3)).reshape(wide_size, 2 * part * chunk)
    wide_parts = lax.all_to_all(band_sum, "wide", 0, 0, tiled=True)
    share = jnp.sum(wide_parts, axis=0, keepdims=True)
    joined = lax.all_to_all(
        jnp.broadcast_to(share, (band_count,) + share.shape[1:]), "rows", 0, 0, tiled=True
    )
    joined = joined.reshape(band_count, 2, part, chunk)
    joined = jnp.transpose(joined, (1, 3, 0, 2)).reshape(2, chunk, channels)
    return joined[0], joined[1]


def tap_patches(padded, frames, rows, cols):
    taps = [
        padded[a : a + frames, b : b + rows, e : e + cols]
        for a in range(3)
        for b in range(3)
        for e in range(3)
    ]
    stacked = jnp.stack(taps, axis=3)
    return stacked.reshape(frames * rows * cols, 27 * padded.shape[-1])


def forward_patches(extended):
    frames, rows_ext, cols, _ = extended.shape
    padded = jnp.concatenate([extended[:1], extended[:1], extended], axis=0)
    padded = jnp.pad(padded, ((0, 0), (0, 0), (1, 1), (0, 0)))
    return tap_patches(padded, frames, rows_ext - 2, cols)


def conv_out(patches, kernel_t, shape):
    result = lax.dot_general(
        patches, kernel_t, (((1,), (1,)), ((), ())), preferred_element_type=jnp.float32
    )
    return result.reshape(shape)


def weight_grad_t(patches, upstream):
    flat = upstream.reshape(-1, upstream.shape[-1])
    return lax.dot_general(
        flat, patches, (((0,), (0,)), ((), ())), preferred_element_type=jnp.float32
    )


def data_grad(upstream_ext, kernel_t):
    frames, rows_ext, cols, _ = upstream_ext.shape
    rows = rows_ext - 2
    padded = jnp.pad(upstream_ext, ((2, 2), (0, 0), (1, 1), (0, 0)))
    padded = padded[::-1, ::-1, ::-1]
    patches = tap_patches(padded, frames + 2, rows, cols)
    cout = kernel_t.shape[0]
    regrouped = kernel_t.reshape(cout, 27, -1).transpose(1, 0, 2).reshape(27 * cout, -1)
    result = jnp.dot(patches, regrouped, preferred_element_type=jnp.float32)
    result = result.reshape(frames + 2, rows, cols, -1)[::-1, ::-1, ::-1]
    head = (result[0] + result[1] + result[2])[None]
    return jnp.concatenate([head, result[3:]], axis=0)


def body(slabs, dest, pos, lengths, cot, w_first, w_second):
    wide_size = lax.axis_size("wide")
    band_count = lax.axis_size("rows")
    slab_count = slabs.shape[2]
    columns = slabs.shape[3]
    channels = slabs.shape[4]
    frames = cot.shape[1]
    band_rows = cot.shape[2]
    rows_local = w_first.shape[0]
    capacity = -(-slab_count // wide_size)
    slot_count = wide_size * capacity
    targets = dest[0, 0]
    places = pos[0, 0]
    ranking = jnp.arange(slab_count, dtype=jnp.int32)
    earlier = (targets[None, :] == targets[:, None]) & (ranking[None, :] < ranking[:, None])
    slab_rank = jnp.sum(earlier.astype(jnp.int32), axis=1)
    slot_of = targets * capacity + slab_rank
    placing = slot_of[None, :] == jnp.arange(slot_count, dtype=jnp.int32)[:, None]
    flat_slabs = slabs[0, 0].reshape(slab_count, columns * channels)
    outgoing = jnp.dot(placing.astype(jnp.bfloat16), flat_slabs, preferred_element_type=jnp.float32)
    outgoing = outgoing.astype(jnp.bfloat16).reshape(wide_size, capacity * columns * channels)
    labels = jnp.sum(jnp.where(placing, places[None, :] + 1, 0), axis=1) - 1
    labels = labels.reshape(wide_size, capacity).astype(jnp.bfloat16)
    label_block = 64
    pieces = weight_pieces(w_first, w_second, band_count)
    tagged = jnp.concatenate(
        [
            outgoing,
            jnp.repeat(labels, label_block // capacity, axis=1),
            jnp.broadcast_to(pieces[None], (wide_size, pieces.shape[0])),
        ],
        axis=1,
    )
    tagged = lax.all_to_all(tagged, "wide", split_axis=0, concat_axis=0, tiled=True)
    payload = capacity * columns * channels
    arrived = tagged[:, :payload].reshape(slot_count, columns * channels)
    arrived_places = tagged[:, payload : payload + label_block : label_block // capacity]
    arrived_places = arrived_places.astype(jnp.int32).reshape(slot_count)
    kernel_first, kernel_second = assemble_weights(
        tagged[:, payload + label_block :], band_count, rows_local, channels
    )
    settle = arrived_places[None, :] == jnp.arange(slab_count, dtype=jnp.int32)[:, None]
    tile = jnp.dot(settle.astype(jnp.bfloat16), arrived, preferred_element_type=jnp.float32)
    tile = tile.astype(jnp.bfloat16).reshape(frames, band_rows, columns, channels)
    field = (frames, band_rows, columns, channels)
    tile_wide = tile.astype(jnp.float32)
    first = jax.nn.silu(tile_wide).astype(jnp.bfloat16)
    first_ext = with_halo(first, (("rows", 1),), 1)
    first_patches = forward_patches(first_ext)
    act = conv_out(first_patches, kernel_first, field).astype(jnp.bfloat16)
    second = jax.nn.silu(act.astype(jnp.float32)).astype(jnp.bfloat16)
    second_ext = with_halo(second, (("rows", 1),), 1)
    second_patches = forward_patches(second_ext)
    block_out = (tile_wide + conv_out(second_patches, kernel_second, field)).astype(jnp.bfloat16)
    live = (jnp.arange(frames, dtype=jnp.int32) < lengths[0])[:, None, None, None]
    out_grad = jnp.where(live, cot[0], jnp.zeros_like(cot[0]))
    out_grad_ext = with_halo(out_grad, (("rows", 1),), 1)
    weight_second = weight_grad_t(second_patches, out_grad)
    hidden_grad = data_grad(out_grad_ext, kernel_second)
    act_grad = (hidden_grad * silu_slope(act.astype(jnp.float32))).astype(jnp.bfloat16)
    act_grad_ext = with_halo(act_grad, (("rows", 1),), 1)
    weight_first = weight_grad_t(first_patches, act_grad)
    first_grad = data_grad(act_grad_ext, kernel_first)
    grad_input = (out_grad.astype(jnp.float32) + first_grad * silu_slope(tile_wide)).astype(
        jnp.bfloat16
    )
    scale = 1.0 / math.sqrt(frames * band_rows * columns * band_count * wide_size)
    grads = jnp.stack([weight_first, weight_second]) * scale
    share_first, share_second = reduce_weight_grads(grads, band_count, wide_size)
    return (block_out[None], grad_input[None], share_first, share_second)


def solution(mesh):

    return jax.shard_map(
        body,
        mesh=mesh,
        in_specs=(
            P("wide", "rows", None, None, None),
            P("wide", "rows", None),
            P("wide", "rows", None),
            P("wide"),
            P("wide", None, "rows", None, None),
            P("wide", None),
            P("wide", None),
        ),
        out_specs=(
            P("wide", None, "rows", None, None),
            P("wide", None, "rows", None, None),
            P("wide", None),
            P("wide", None),
        ),
        check_vma=False,
    )
```

```python
import math

import jax
import jax.numpy as jnp
from jax import lax
from jax.sharding import PartitionSpec as P


def with_halo(block, sides, width):
    for axis, dim in sides:
        count = lax.axis_size(axis)
        forward = [(i, i + 1) for i in range(count - 1)]
        backward = [(target, source) for source, target in forward]
        low = lax.ppermute(
            lax.slice_in_dim(block, block.shape[dim] - width, None, axis=dim), axis, forward
        )
        high = lax.ppermute(lax.slice_in_dim(block, 0, width, axis=dim), axis, backward)
        block = jnp.concatenate([low, block, high], axis=dim)
    return block


def silu_slope(values):
    sig = jax.nn.sigmoid(values)
    return sig * (1.0 + values * (1.0 - sig))


def gather_weights(w_first, w_second, band_count):
    rows_local, channels = w_first.shape
    part = channels // band_count
    wide_size = lax.axis_size("wide")
    me = lax.axis_index("rows")
    both = jnp.stack([w_first, w_second])
    mine = lax.dynamic_slice_in_dim(both, me * part, part, axis=2)
    mine = jnp.transpose(mine, (0, 2, 1)).reshape(1, 2 * part * rows_local)
    spread = jnp.broadcast_to(mine, (wide_size * band_count, mine.shape[1]))
    pieces = lax.all_to_all(spread, ("wide", "rows"), 0, 0, tiled=True)
    pieces = pieces.reshape(wide_size, band_count, 2, part, rows_local)
    full = jnp.transpose(pieces, (2, 1, 3, 0, 4)).reshape(2, channels, wide_size * rows_local)
    return full[0], full[1]


def reduce_weight_grads(grad_t, band_count, wide_size):
    _, channels, total_rows = grad_t.shape
    part = channels // band_count
    chunk = total_rows // wide_size
    blocks = grad_t.astype(jnp.bfloat16).reshape(2, band_count, part, wide_size, chunk)
    blocks = jnp.transpose(blocks, (3, 1, 0, 2, 4)).reshape(wide_size * band_count, 2 * part * chunk)
    parts = lax.all_to_all(blocks, ("wide", "rows"), 0, 0, tiled=True)
    share = jnp.sum(parts.astype(jnp.float32), axis=0, keepdims=True)
    joined = lax.all_to_all(
        jnp.broadcast_to(share, (band_count,) + share.shape[1:]), "rows", 0, 0, tiled=True
    )
    joined = joined.reshape(band_count, 2, part, chunk)
    joined = jnp.transpose(joined, (1, 3, 0, 2)).reshape(2, chunk, channels)
    return joined[0], joined[1]


def tap_patches(padded, frames, rows, cols):
    taps = [
        padded[a : a + frames, b : b + rows, e : e + cols]
        for a in range(3)
        for b in range(3)
        for e in range(3)
    ]
    stacked = jnp.stack(taps, axis=3)
    return stacked.reshape(frames * rows * cols, 27 * padded.shape[-1])


def forward_patches(extended):
    frames, rows_ext, cols, _ = extended.shape
    padded = jnp.concatenate([extended[:1], extended[:1], extended], axis=0)
    padded = jnp.pad(padded, ((0, 0), (0, 0), (1, 1), (0, 0)))
    return tap_patches(padded, frames, rows_ext - 2, cols)


def conv_out(patches, kernel_t, shape):
    result = lax.dot_general(
        patches, kernel_t, (((1,), (1,)), ((), ())), preferred_element_type=jnp.float32
    )
    return result.reshape(shape)


def weight_grad_t(patches, upstream):
    flat = upstream.reshape(-1, upstream.shape[-1])
    return lax.dot_general(
        flat, patches, (((0,), (0,)), ((), ())), preferred_element_type=jnp.float32
    )


def data_grad(upstream_ext, kernel_t):
    frames, rows_ext, cols, _ = upstream_ext.shape
    rows = rows_ext - 2
    padded = jnp.pad(upstream_ext, ((2, 2), (0, 0), (1, 1), (0, 0)))
    padded = padded[::-1, ::-1, ::-1]
    patches = tap_patches(padded, frames + 2, rows, cols)
    cout = kernel_t.shape[0]
    regrouped = kernel_t.reshape(cout, 27, -1).transpose(1, 0, 2).reshape(27 * cout, -1)
    result = jnp.dot(patches, regrouped, preferred_element_type=jnp.float32)
    result = result.reshape(frames + 2, rows, cols, -1)[::-1, ::-1, ::-1]
    head = (result[0] + result[1] + result[2])[None]
    return jnp.concatenate([head, result[3:]], axis=0)


def body(slabs, dest, pos, lengths, cot, w_first, w_second):
    wide_size = lax.axis_size("wide")
    band_count = lax.axis_size("rows")
    slab_count = slabs.shape[2]
    columns = slabs.shape[3]
    channels = slabs.shape[4]
    frames = cot.shape[1]
    band_rows = cot.shape[2]
    rows_local = w_first.shape[0]
    capacity = -(-slab_count // wide_size)
    slot_count = wide_size * capacity
    targets = dest[0, 0]
    places = pos[0, 0]
    ranking = jnp.arange(slab_count, dtype=jnp.int32)
    earlier = (targets[None, :] == targets[:, None]) & (ranking[None, :] < ranking[:, None])
    slab_rank = jnp.sum(earlier.astype(jnp.int32), axis=1)
    slot_of = targets * capacity + slab_rank
    placing = slot_of[None, :] == jnp.arange(slot_count, dtype=jnp.int32)[:, None]
    flat_slabs = slabs[0, 0].reshape(slab_count, columns * channels)
    outgoing = jnp.dot(placing.astype(jnp.bfloat16), flat_slabs, preferred_element_type=jnp.float32)
    outgoing = outgoing.astype(jnp.bfloat16).reshape(wide_size, capacity * columns * channels)
    labels = jnp.sum(jnp.where(placing, places[None, :] + 1, 0), axis=1) - 1
    labels = labels.reshape(wide_size, capacity).astype(jnp.bfloat16)
    label_block = 128
    tagged = jnp.concatenate(
        [outgoing, jnp.repeat(labels, label_block // capacity, axis=1)], axis=1
    )
    tagged = lax.all_to_all(tagged, "wide", split_axis=0, concat_axis=0, tiled=True)
    payload = capacity * columns * channels
    arrived = tagged[:, :payload].reshape(slot_count, columns * channels)
    arrived_places = tagged[:, payload : payload + label_block : label_block // capacity]
    arrived_places = arrived_places.astype(jnp.int32).reshape(slot_count)
    kernel_first, kernel_second = gather_weights(w_first, w_second, band_count)
    settle = arrived_places[None, :] == jnp.arange(slab_count, dtype=jnp.int32)[:, None]
    tile = jnp.dot(settle.astype(jnp.bfloat16), arrived, preferred_element_type=jnp.float32)
    tile = tile.astype(jnp.bfloat16).reshape(frames, band_rows, columns, channels)
    field = (frames, band_rows, columns, channels)
    tile_wide = tile.astype(jnp.float32)
    first = jax.nn.silu(tile_wide).astype(jnp.bfloat16)
    first_ext = with_halo(first, (("rows", 1),), 1)
    first_patches = forward_patches(first_ext)
    act = conv_out(first_patches, kernel_first, field).astype(jnp.bfloat16)
    second = jax.nn.silu(act.astype(jnp.float32)).astype(jnp.bfloat16)
    second_ext = with_halo(second, (("rows", 1),), 1)
    second_patches = forward_patches(second_ext)
    block_out = (tile_wide + conv_out(second_patches, kernel_second, field)).astype(jnp.bfloat16)
    live = (jnp.arange(frames, dtype=jnp.int32) < lengths[0])[:, None, None, None]
    out_grad = jnp.where(live, cot[0], jnp.zeros_like(cot[0]))
    out_grad_ext = with_halo(out_grad, (("rows", 1),), 1)
    weight_second = weight_grad_t(second_patches, out_grad)
    hidden_grad = data_grad(out_grad_ext, kernel_second)
    act_grad = (hidden_grad * silu_slope(act.astype(jnp.float32))).astype(jnp.bfloat16)
    act_grad_ext = with_halo(act_grad, (("rows", 1),), 1)
    weight_first = weight_grad_t(first_patches, act_grad)
    first_grad = data_grad(act_grad_ext, kernel_first)
    grad_input = (out_grad.astype(jnp.float32) + first_grad * silu_slope(tile_wide)).astype(
        jnp.bfloat16
    )
    scale = 1.0 / math.sqrt(frames * band_rows * columns * band_count * wide_size)
    grads = jnp.stack([weight_first, weight_second]) * scale
    share_first, share_second = reduce_weight_grads(grads, band_count, wide_size)
    return (block_out[None], grad_input[None], share_first, share_second)


def solution(mesh):

    return jax.shard_map(
        body,
        mesh=mesh,
        in_specs=(
            P("wide", "rows", None, None, None),
            P("wide", "rows", None),
            P("wide", "rows", None),
            P("wide"),
            P("wide", None, "rows", None, None),
            P("wide", None),
            P("wide", None),
        ),
        out_specs=(
            P("wide", None, "rows", None, None),
            P("wide", None, "rows", None, None),
            P("wide", None),
            P("wide", None),
        ),
        check_vma=False,
    )
```

```python
import math

import jax
import jax.numpy as jnp
from jax import lax
from jax.sharding import PartitionSpec as P


def with_halo(block, sides, width):
    for axis, dim in sides:
        count = lax.axis_size(axis)
        forward = [(i, i + 1) for i in range(count - 1)]
        backward = [(target, source) for source, target in forward]
        low = lax.ppermute(
            lax.slice_in_dim(block, block.shape[dim] - width, None, axis=dim), axis, forward
        )
        high = lax.ppermute(lax.slice_in_dim(block, 0, width, axis=dim), axis, backward)
        block = jnp.concatenate([low, block, high], axis=dim)
    return block


def silu_slope(values):
    sig = jax.nn.sigmoid(values)
    return sig * (1.0 + values * (1.0 - sig))


def weight_pieces(w_first, w_second, band_count):
    rows_local, channels = w_first.shape
    part = channels // band_count
    me = lax.axis_index("rows")
    both = jnp.stack([w_first, w_second])
    mine = lax.dynamic_slice_in_dim(both, me * part, part, axis=2)
    return jnp.transpose(mine, (0, 2, 1)).reshape(2 * part * rows_local)


def assemble_weights(pieces, band_count, rows_local, channels):
    count = pieces.shape[0]
    part = channels // band_count
    block = pieces.reshape(count, 2, part, rows_local)
    block = jnp.transpose(block, (1, 2, 0, 3)).reshape(2, part, count * rows_local)
    full = lax.all_gather(block, "rows", axis=1, tiled=True)
    return full[0], full[1]


def reduce_weight_grads(grad_t, band_count, wide_size):
    _, channels, total_rows = grad_t.shape
    part = channels // band_count
    chunk = total_rows // wide_size
    blocks = grad_t.astype(jnp.bfloat16).reshape(2, band_count, part, total_rows)
    blocks = jnp.transpose(blocks, (1, 0, 2, 3))
    band_parts = lax.all_to_all(blocks, "rows", 0, 0, tiled=True)
    band_sum = jnp.sum(band_parts.astype(jnp.float32), axis=0)
    band_sum = band_sum.reshape(2, part, wide_size, chunk)
    band_sum = jnp.transpose(band_sum, (2, 0, 1, 3)).reshape(wide_size, 2 * part * chunk)
    wide_parts = lax.all_to_all(band_sum, "wide", 0, 0, tiled=True)
    share = jnp.sum(wide_parts, axis=0, keepdims=True)
    joined = lax.all_to_all(
        jnp.broadcast_to(share, (band_count,) + share.shape[1:]), "rows", 0, 0, tiled=True
    )
    joined = joined.reshape(band_count, 2, part, chunk)
    joined = jnp.transpose(joined, (1, 3, 0, 2)).reshape(2, chunk, channels)
    return joined[0], joined[1]


def conv_forward_t(extended, kernel_t):
    cout = kernel_t.shape[0]
    kernel = kernel_t.reshape(cout, 3, 3, 3, -1)
    padded = jnp.concatenate([extended[:1], extended[:1], extended], axis=0)
    result = lax.conv_general_dilated(
        padded[None], kernel, (1, 1, 1), ((0, 0), (0, 0), (1, 1)),
        dimension_numbers=("NDHWC", "ODHWI", "NDHWC"), preferred_element_type=jnp.float32,
    )
    return result[0]


def conv_weight_grad_t(extended, upstream):
    padded = jnp.concatenate([extended[:1], extended[:1], extended], axis=0)
    result = lax.conv_general_dilated(
        padded[None], upstream[None], (1, 1, 1), ((0, 0), (0, 0), (1, 1)),
        dimension_numbers=("CDHWN", "IDHWO", "CDHWN"), preferred_element_type=jnp.float32,
    )
    return result.reshape(upstream.shape[-1], -1)


def conv_data_grad_t(upstream_ext, kernel_t):
    cout = kernel_t.shape[0]
    kernel = kernel_t.reshape(cout, 3, 3, 3, -1)[:, ::-1, ::-1, ::-1, :]
    padded = jnp.pad(upstream_ext, ((2, 2), (0, 0), (0, 0), (0, 0)))
    result = lax.conv_general_dilated(
        padded[None], kernel, (1, 1, 1), ((0, 0), (0, 0), (1, 1)),
        dimension_numbers=("NDHWC", "IDHWO", "NDHWC"), preferred_element_type=jnp.float32,
    )[0]
    head = (result[0] + result[1] + result[2])[None]
    return jnp.concatenate([head, result[3:]], axis=0)


def body(slabs, dest, pos, lengths, cot, w_first, w_second):
    wide_size = lax.axis_size("wide")
    band_count = lax.axis_size("rows")
    slab_count = slabs.shape[2]
    columns = slabs.shape[3]
    channels = slabs.shape[4]
    frames = cot.shape[1]
    band_rows = cot.shape[2]
    rows_local = w_first.shape[0]
    capacity = -(-slab_count // wide_size)
    slot_count = wide_size * capacity
    targets = dest[0, 0]
    places = pos[0, 0]
    ranking = jnp.arange(slab_count, dtype=jnp.int32)
    earlier = (targets[None, :] == targets[:, None]) & (ranking[None, :] < ranking[:, None])
    slab_rank = jnp.sum(earlier.astype(jnp.int32), axis=1)
    slot_of = targets * capacity + slab_rank
    placing = slot_of[None, :] == jnp.arange(slot_count, dtype=jnp.int32)[:, None]
    flat_slabs = slabs[0, 0].reshape(slab_count, columns * channels)
    outgoing = jnp.dot(placing.astype(jnp.bfloat16), flat_slabs, preferred_element_type=jnp.float32)
    outgoing = outgoing.astype(jnp.bfloat16).reshape(wide_size, capacity * columns * channels)
    labels = jnp.sum(jnp.where(placing, places[None, :] + 1, 0), axis=1) - 1
    labels = labels.reshape(wide_size, capacity).astype(jnp.bfloat16)
    label_block = 128
    pieces = weight_pieces(w_first, w_second, band_count)
    pieces = lax.all_to_all(
        jnp.broadcast_to(pieces[None], (wide_size, pieces.shape[0])), "wide", 0, 0, tiled=True
    )
    kernel_first, kernel_second = assemble_weights(pieces, band_count, rows_local, channels)
    tagged = jnp.concatenate(
        [outgoing, jnp.repeat(labels, label_block // capacity, axis=1)], axis=1
    )
    tagged = lax.all_to_all(tagged, "wide", split_axis=0, concat_axis=0, tiled=True)
    payload = capacity * columns * channels
    arrived = tagged[:, :payload].reshape(slot_count, columns * channels)
    arrived_places = tagged[:, payload : payload + label_block : label_block // capacity]
    arrived_places = arrived_places.astype(jnp.int32).reshape(slot_count)
    settle = arrived_places[None, :] == jnp.arange(slab_count, dtype=jnp.int32)[:, None]
    tile = jnp.dot(settle.astype(jnp.bfloat16), arrived, preferred_element_type=jnp.float32)
    tile = tile.astype(jnp.bfloat16).reshape(frames, band_rows, columns, channels)
    tile_wide = tile.astype(jnp.float32)
    first = jax.nn.silu(tile_wide).astype(jnp.bfloat16)
    first_ext = with_halo(first, (("rows", 1),), 1)
    act = conv_forward_t(first_ext, kernel_first).astype(jnp.bfloat16)
    second = jax.nn.silu(act.astype(jnp.float32)).astype(jnp.bfloat16)
    second_ext = with_halo(second, (("rows", 1),), 1)
    block_out = (tile_wide + conv_forward_t(second_ext, kernel_second)).astype(jnp.bfloat16)
    live = (jnp.arange(frames, dtype=jnp.int32) < lengths[0])[:, None, None, None]
    out_grad = jnp.where(live, cot[0], jnp.zeros_like(cot[0]))
    out_grad_ext = with_halo(out_grad, (("rows", 1),), 1)
    weight_second = conv_weight_grad_t(second_ext, out_grad)
    hidden_grad = conv_data_grad_t(out_grad_ext, kernel_second)
    act_grad = (hidden_grad * silu_slope(act.astype(jnp.float32))).astype(jnp.bfloat16)
    act_grad_ext = with_halo(act_grad, (("rows", 1),), 1)
    weight_first = conv_weight_grad_t(first_ext, act_grad)
    first_grad = conv_data_grad_t(act_grad_ext, kernel_first)
    grad_input = (out_grad.astype(jnp.float32) + first_grad * silu_slope(tile_wide)).astype(
        jnp.bfloat16
    )
    scale = 1.0 / math.sqrt(frames * band_rows * columns * band_count * wide_size)
    grads = jnp.stack([weight_first, weight_second]) * scale
    share_first, share_second = reduce_weight_grads(grads, band_count, wide_size)
    return (block_out[None], grad_input[None], share_first, share_second)


def solution(mesh):

    return jax.shard_map(
        body,
        mesh=mesh,
        in_specs=(
            P("wide", "rows", None, None, None),
            P("wide", "rows", None),
            P("wide", "rows", None),
            P("wide"),
            P("wide", None, "rows", None, None),
            P("wide", None),
            P("wide", None),
        ),
        out_specs=(
            P("wide", None, "rows", None, None),
            P("wide", None, "rows", None, None),
            P("wide", None),
            P("wide", None),
        ),
        check_vma=False,
    )
```

```python
import math

import jax
import jax.numpy as jnp
from jax import lax
from jax.sharding import PartitionSpec as P


def with_halo(block, sides, width):
    for axis, dim in sides:
        count = lax.axis_size(axis)
        forward = [(i, i + 1) for i in range(count - 1)]
        backward = [(target, source) for source, target in forward]
        low = lax.ppermute(
            lax.slice_in_dim(block, block.shape[dim] - width, None, axis=dim), axis, forward
        )
        high = lax.ppermute(lax.slice_in_dim(block, 0, width, axis=dim), axis, backward)
        block = jnp.concatenate([low, block, high], axis=dim)
    return block


def silu_slope(values):
    sig = jax.nn.sigmoid(values)
    return sig * (1.0 + values * (1.0 - sig))


def reduce_weight_grads(grad_t, band_count, wide_size):
    _, channels, total_rows = grad_t.shape
    part = channels // band_count
    chunk = total_rows // wide_size
    blocks = grad_t.astype(jnp.bfloat16).reshape(2, band_count, part, total_rows)
    blocks = jnp.transpose(blocks, (1, 0, 2, 3))
    band_parts = lax.all_to_all(blocks, "rows", 0, 0, tiled=True)
    band_sum = jnp.sum(band_parts.astype(jnp.float32), axis=0)
    band_sum = band_sum.reshape(2, part, wide_size, chunk)
    band_sum = jnp.transpose(band_sum, (2, 0, 1, 3)).reshape(wide_size, 2 * part * chunk)
    wide_parts = lax.all_to_all(band_sum, "wide", 0, 0, tiled=True)
    share = jnp.sum(wide_parts, axis=0, keepdims=True)
    joined = lax.all_to_all(
        jnp.broadcast_to(share, (band_count,) + share.shape[1:]), "rows", 0, 0, tiled=True
    )
    joined = joined.reshape(band_count, 2, part, chunk)
    joined = jnp.transpose(joined, (1, 3, 0, 2)).reshape(2, chunk, channels)
    return joined[0], joined[1]


def conv_forward(extended, kernel):
    padded = jnp.concatenate([extended[:1], extended[:1], extended], axis=0)
    result = lax.conv_general_dilated(
        padded[None], kernel, (1, 1, 1), ((0, 0), (0, 0), (1, 1)),
        dimension_numbers=("NDHWC", "DHWIO", "NDHWC"), preferred_element_type=jnp.float32,
    )
    return result[0]


def conv_data_grad(upstream_ext, kernel):
    padded = jnp.pad(upstream_ext, ((2, 2), (0, 0), (0, 0), (0, 0)))
    flipped = kernel[::-1, ::-1, ::-1]
    result = lax.conv_general_dilated(
        padded[None], flipped, (1, 1, 1), ((0, 0), (0, 0), (1, 1)),
        dimension_numbers=("NDHWC", "DHWOI", "NDHWC"), preferred_element_type=jnp.float32,
    )[0]
    head = (result[0] + result[1] + result[2])[None]
    return jnp.concatenate([head, result[3:]], axis=0)


def conv_weight_grad_t(extended, upstream):
    padded = jnp.concatenate([extended[:1], extended[:1], extended], axis=0)
    result = lax.conv_general_dilated(
        padded[None], upstream[None], (1, 1, 1), ((0, 0), (0, 0), (1, 1)),
        dimension_numbers=("CDHWN", "IDHWO", "CDHWN"), preferred_element_type=jnp.float32,
    )
    return result.reshape(upstream.shape[-1], -1)


def body(slabs, dest, pos, lengths, cot, w_first, w_second):
    wide_size = lax.axis_size("wide")
    band_count = lax.axis_size("rows")
    slab_count = slabs.shape[2]
    columns = slabs.shape[3]
    channels = slabs.shape[4]
    frames = cot.shape[1]
    band_rows = cot.shape[2]
    rows_local = w_first.shape[0]
    capacity = -(-slab_count // wide_size)
    slot_count = wide_size * capacity
    targets = dest[0, 0]
    places = pos[0, 0]
    ranking = jnp.arange(slab_count, dtype=jnp.int32)
    earlier = (targets[None, :] == targets[:, None]) & (ranking[None, :] < ranking[:, None])
    slab_rank = jnp.sum(earlier.astype(jnp.int32), axis=1)
    slot_of = targets * capacity + slab_rank
    placing = slot_of[None, :] == jnp.arange(slot_count, dtype=jnp.int32)[:, None]
    flat_slabs = slabs[0, 0].reshape(slab_count, columns * channels)
    outgoing = jnp.dot(placing.astype(jnp.bfloat16), flat_slabs, preferred_element_type=jnp.float32)
    outgoing = outgoing.astype(jnp.bfloat16).reshape(wide_size, capacity * columns * channels)
    labels = jnp.sum(jnp.where(placing, places[None, :] + 1, 0), axis=1) - 1
    labels = labels.reshape(wide_size, capacity).astype(jnp.bfloat16)
    label_block = 128
    chunk_both = jnp.stack([w_first, w_second]).reshape(1, 2 * rows_local * channels)
    tagged = jnp.concatenate(
        [
            outgoing,
            jnp.repeat(labels, label_block // capacity, axis=1),
            jnp.broadcast_to(chunk_both, (wide_size, chunk_both.shape[1])),
        ],
        axis=1,
    )
    tagged = lax.all_to_all(tagged, "wide", split_axis=0, concat_axis=0, tiled=True)
    payload = capacity * columns * channels
    arrived = tagged[:, :payload].reshape(slot_count, columns * channels)
    arrived_places = tagged[:, payload : payload + label_block : label_block // capacity]
    arrived_places = arrived_places.astype(jnp.int32).reshape(slot_count)
    weights = tagged[:, payload + label_block :].reshape(wide_size, 2, rows_local, channels)
    weights = jnp.transpose(weights, (1, 0, 2, 3)).reshape(2, 3, 3, 3, channels, channels)
    kernel_first, kernel_second = weights[0], weights[1]
    settle = arrived_places[None, :] == jnp.arange(slab_count, dtype=jnp.int32)[:, None]
    tile = jnp.dot(settle.astype(jnp.bfloat16), arrived, preferred_element_type=jnp.float32)
    tile = tile.astype(jnp.bfloat16).reshape(frames, band_rows, columns, channels)
    tile_wide = tile.astype(jnp.float32)
    first = jax.nn.silu(tile_wide).astype(jnp.bfloat16)
    first_ext = with_halo(first, (("rows", 1),), 1)
    act = conv_forward(first_ext, kernel_first).astype(jnp.bfloat16)
    second = jax.nn.silu(act.astype(jnp.float32)).astype(jnp.bfloat16)
    second_ext = with_halo(second, (("rows", 1),), 1)
    block_out = (tile_wide + conv_forward(second_ext, kernel_second)).astype(jnp.bfloat16)
    live = (jnp.arange(frames, dtype=jnp.int32) < lengths[0])[:, None, None, None]
    out_grad = jnp.where(live, cot[0], jnp.zeros_like(cot[0]))
    out_grad_ext = with_halo(out_grad, (("rows", 1),), 1)
    weight_second = conv_weight_grad_t(second_ext, out_grad)
    hidden_grad = conv_data_grad(out_grad_ext, kernel_second)
    act_grad = (hidden_grad * silu_slope(act.astype(jnp.float32))).astype(jnp.bfloat16)
    act_grad_ext = with_halo(act_grad, (("rows", 1),), 1)
    weight_first = conv_weight_grad_t(first_ext, act_grad)
    first_grad = conv_data_grad(act_grad_ext, kernel_first)
    grad_input = (out_grad.astype(jnp.float32) + first_grad * silu_slope(tile_wide)).astype(
        jnp.bfloat16
    )
    scale = 1.0 / math.sqrt(frames * band_rows * columns * band_count * wide_size)
    grads = jnp.stack([weight_first, weight_second]) * scale
    share_first, share_second = reduce_weight_grads(grads, band_count, wide_size)
    return (block_out[None], grad_input[None], share_first, share_second)


def solution(mesh):

    return jax.shard_map(
        body,
        mesh=mesh,
        in_specs=(
            P("wide", "rows", None, None, None),
            P("wide", "rows", None),
            P("wide", "rows", None),
            P("wide"),
            P("wide", None, "rows", None, None),
            P("wide", None),
            P("wide", None),
        ),
        out_specs=(
            P("wide", None, "rows", None, None),
            P("wide", None, "rows", None, None),
            P("wide", None),
            P("wide", None),
        ),
        check_vma=False,
    )
```

```python
import functools
import math


import jax
import jax.numpy as jnp
from jax import lax
from jax.experimental import pallas as pl
from jax.experimental.pallas import tpu as pltpu
from jax.sharding import PartitionSpec as P


def with_halo(block, sides, width):
    for axis, dim in sides:
        count = lax.axis_size(axis)
        forward = [(i, i + 1) for i in range(count - 1)]
        backward = [(target, source) for source, target in forward]
        low = lax.ppermute(
            lax.slice_in_dim(block, block.shape[dim] - width, None, axis=dim), axis, forward
        )
        high = lax.ppermute(lax.slice_in_dim(block, 0, width, axis=dim), axis, backward)
        block = jnp.concatenate([low, block, high], axis=dim)
    return block


def silu_slope(values):
    sig = jax.nn.sigmoid(values)
    return sig * (1.0 + values * (1.0 - sig))


def weight_pieces(w_first, w_second, band_count):
    rows_local, channels = w_first.shape
    part = channels // band_count
    me = lax.axis_index("rows")
    both = jnp.stack([w_first, w_second])
    mine = lax.dynamic_slice_in_dim(both, me * part, part, axis=2)
    return jnp.transpose(mine, (0, 2, 1)).reshape(2 * part * rows_local)


def assemble_weights(pieces, band_count, rows_local, channels):
    count = pieces.shape[0]
    part = channels // band_count
    block = pieces.reshape(count, 2, part, rows_local)
    block = jnp.transpose(block, (1, 2, 0, 3)).reshape(2, part, count * rows_local)
    full = lax.all_gather(block, "rows", axis=1, tiled=True)
    return full[0], full[1]


def _wide_sum_kernel(count, x_ref, o_ref, recv, send_sems, recv_sems):
    me = lax.axis_index("wide")
    band = lax.axis_index("rows")
    barrier = pltpu.get_barrier_semaphore()

    def greet(k, carry):
        peer = lax.rem(me + k, count)
        pl.semaphore_signal(
            barrier, 1, device_id=(peer, band), device_id_type=pl.DeviceIdType.MESH
        )
        return carry

    lax.fori_loop(1, count, greet, 0)
    pl.semaphore_wait(barrier, count - 1)

    def send(k, carry):
        peer = lax.rem(me + k, count)
        pltpu.make_async_remote_copy(
            src_ref=x_ref.at[peer],
            dst_ref=recv.at[me],
            send_sem=send_sems.at[peer],
            recv_sem=recv_sems.at[me],
            device_id=(peer, band),
            device_id_type=pl.DeviceIdType.MESH,
        ).start()
        return carry

    lax.fori_loop(1, count, send, 0)

    def finish(k, total):
        peer = lax.rem(me + k, count)
        source = lax.rem(me + count - k, count)
        pltpu.make_async_remote_copy(
            src_ref=x_ref.at[peer],
            dst_ref=recv.at[me],
            send_sem=send_sems.at[peer],
            recv_sem=recv_sems.at[me],
            device_id=(peer, band),
            device_id_type=pl.DeviceIdType.MESH,
        ).wait_send()
        pltpu.make_async_remote_copy(
            src_ref=x_ref.at[source],
            dst_ref=recv.at[source],
            send_sem=send_sems.at[source],
            recv_sem=recv_sems.at[source],
            device_id=(source, band),
            device_id_type=pl.DeviceIdType.MESH,
        ).wait_recv()
        return total + recv[source]

    total = lax.fori_loop(1, count, finish, x_ref[me])
    o_ref[...] = total


def wide_sum(pieces):
    count = pieces.shape[0]
    return pl.pallas_call(
        functools.partial(_wide_sum_kernel, count),
        out_shape=jax.ShapeDtypeStruct(pieces.shape[1:], pieces.dtype),
        in_specs=[pl.BlockSpec(memory_space=pltpu.VMEM)],
        out_specs=pl.BlockSpec(memory_space=pltpu.VMEM),
        scratch_shapes=[
            pltpu.VMEM(pieces.shape, pieces.dtype),
            pltpu.SemaphoreType.DMA((count,)),
            pltpu.SemaphoreType.DMA((count,)),
        ],
        compiler_params=pltpu.CompilerParams(collective_id=0, has_side_effects=True),
    )(pieces)


def reduce_weight_grads(grad_t, band_count, wide_size):
    _, channels, total_rows = grad_t.shape
    part = channels // band_count
    chunk = total_rows // wide_size
    blocks = grad_t.astype(jnp.bfloat16).reshape(2, band_count, part, total_rows)
    blocks = jnp.transpose(blocks, (1, 0, 2, 3))
    band_parts = lax.all_to_all(blocks, "rows", 0, 0, tiled=True)
    band_sum = jnp.sum(band_parts.astype(jnp.float32), axis=0)
    band_sum = band_sum.reshape(2, part, wide_size, chunk)
    band_sum = jnp.transpose(band_sum, (2, 0, 1, 3)).reshape(wide_size, 2 * part * chunk)
    size = band_sum.shape[1]
    lanes = 128
    tall = -(-size // (8 * lanes)) * 8
    padded = jnp.pad(band_sum, ((0, 0), (0, tall * lanes - size)))
    share = wide_sum(padded.reshape(wide_size, tall, lanes)).reshape(1, tall * lanes)[:, :size]
    joined = lax.all_to_all(
        jnp.broadcast_to(share, (band_count,) + share.shape[1:]), "rows", 0, 0, tiled=True
    )
    joined = joined.reshape(band_count, 2, part, chunk)
    joined = jnp.transpose(joined, (1, 3, 0, 2)).reshape(2, chunk, channels)
    return joined[0], joined[1]


def conv_forward_t(extended, kernel_t):
    cout = kernel_t.shape[0]
    kernel = kernel_t.reshape(cout, 3, 3, 3, -1)
    padded = jnp.concatenate([extended[:1], extended[:1], extended], axis=0)
    result = lax.conv_general_dilated(
        padded[None], kernel, (1, 1, 1), ((0, 0), (0, 0), (1, 1)),
        dimension_numbers=("NDHWC", "ODHWI", "NDHWC"), preferred_element_type=jnp.float32,
    )
    return result[0]


def conv_weight_grad_t(extended, upstream):
    padded = jnp.concatenate([extended[:1], extended[:1], extended], axis=0)
    result = lax.conv_general_dilated(
        padded[None], upstream[None], (1, 1, 1), ((0, 0), (0, 0), (1, 1)),
        dimension_numbers=("CDHWN", "IDHWO", "CDHWN"), preferred_element_type=jnp.float32,
    )
    return result.reshape(upstream.shape[-1], -1)


def conv_data_grad_t(upstream_ext, kernel_t):
    cout = kernel_t.shape[0]
    kernel = kernel_t.reshape(cout, 3, 3, 3, -1)[:, ::-1, ::-1, ::-1, :]
    padded = jnp.pad(upstream_ext, ((2, 2), (0, 0), (0, 0), (0, 0)))
    result = lax.conv_general_dilated(
        padded[None], kernel, (1, 1, 1), ((0, 0), (0, 0), (1, 1)),
        dimension_numbers=("NDHWC", "IDHWO", "NDHWC"), preferred_element_type=jnp.float32,
    )[0]
    head = (result[0] + result[1] + result[2])[None]
    return jnp.concatenate([head, result[3:]], axis=0)


def body(slabs, dest, pos, lengths, cot, w_first, w_second):
    wide_size = lax.axis_size("wide")
    band_count = lax.axis_size("rows")
    slab_count = slabs.shape[2]
    columns = slabs.shape[3]
    channels = slabs.shape[4]
    frames = cot.shape[1]
    band_rows = cot.shape[2]
    rows_local = w_first.shape[0]
    capacity = -(-slab_count // wide_size)
    slot_count = wide_size * capacity
    targets = dest[0, 0]
    places = pos[0, 0]
    ranking = jnp.arange(slab_count, dtype=jnp.int32)
    earlier = (targets[None, :] == targets[:, None]) & (ranking[None, :] < ranking[:, None])
    slab_rank = jnp.sum(earlier.astype(jnp.int32), axis=1)
    slot_of = targets * capacity + slab_rank
    placing = slot_of[None, :] == jnp.arange(slot_count, dtype=jnp.int32)[:, None]
    flat_slabs = slabs[0, 0].reshape(slab_count, columns * channels)
    outgoing = jnp.dot(placing.astype(jnp.bfloat16), flat_slabs, preferred_element_type=jnp.float32)
    outgoing = outgoing.astype(jnp.bfloat16).reshape(wide_size, capacity * columns * channels)
    labels = jnp.sum(jnp.where(placing, places[None, :] + 1, 0), axis=1) - 1
    labels = labels.reshape(wide_size, capacity).astype(jnp.bfloat16)
    label_block = 128
    pieces = weight_pieces(w_first, w_second, band_count)
    pieces = lax.all_to_all(
        jnp.broadcast_to(pieces[None], (wide_size, pieces.shape[0])), "wide", 0, 0, tiled=True
    )
    kernel_first, kernel_second = assemble_weights(pieces, band_count, rows_local, channels)
    tagged = jnp.concatenate(
        [outgoing, jnp.repeat(labels, label_block // capacity, axis=1)], axis=1
    )
    tagged = lax.all_to_all(tagged, "wide", split_axis=0, concat_axis=0, tiled=True)
    payload = capacity * columns * channels
    arrived = tagged[:, :payload].reshape(slot_count, columns * channels)
    arrived_places = tagged[:, payload : payload + label_block : label_block // capacity]
    arrived_places = arrived_places.astype(jnp.int32).reshape(slot_count)
    settle = arrived_places[None, :] == jnp.arange(slab_count, dtype=jnp.int32)[:, None]
    tile = jnp.dot(settle.astype(jnp.bfloat16), arrived, preferred_element_type=jnp.float32)
    tile = tile.astype(jnp.bfloat16).reshape(frames, band_rows, columns, channels)
    tile_wide = tile.astype(jnp.float32)
    first = jax.nn.silu(tile_wide).astype(jnp.bfloat16)
    first_ext = with_halo(first, (("rows", 1),), 1)
    act = conv_forward_t(first_ext, kernel_first).astype(jnp.bfloat16)
    second = jax.nn.silu(act.astype(jnp.float32)).astype(jnp.bfloat16)
    second_ext = with_halo(second, (("rows", 1),), 1)
    block_out = (tile_wide + conv_forward_t(second_ext, kernel_second)).astype(jnp.bfloat16)
    live = (jnp.arange(frames, dtype=jnp.int32) < lengths[0])[:, None, None, None]
    out_grad = jnp.where(live, cot[0], jnp.zeros_like(cot[0]))
    out_grad_ext = with_halo(out_grad, (("rows", 1),), 1)
    weight_second = conv_weight_grad_t(second_ext, out_grad)
    hidden_grad = conv_data_grad_t(out_grad_ext, kernel_second)
    act_grad = (hidden_grad * silu_slope(act.astype(jnp.float32))).astype(jnp.bfloat16)
    act_grad_ext = with_halo(act_grad, (("rows", 1),), 1)
    weight_first = conv_weight_grad_t(first_ext, act_grad)
    first_grad = conv_data_grad_t(act_grad_ext, kernel_first)
    grad_input = (out_grad.astype(jnp.float32) + first_grad * silu_slope(tile_wide)).astype(
        jnp.bfloat16
    )
    scale = 1.0 / math.sqrt(frames * band_rows * columns * band_count * wide_size)
    grads = jnp.stack([weight_first, weight_second]) * scale
    share_first, share_second = reduce_weight_grads(grads, band_count, wide_size)
    return (block_out[None], grad_input[None], share_first, share_second)


def solution(mesh):

    return jax.shard_map(
        body,
        mesh=mesh,
        in_specs=(
            P("wide", "rows", None, None, None),
            P("wide", "rows", None),
            P("wide", "rows", None),
            P("wide"),
            P("wide", None, "rows", None, None),
            P("wide", None),
            P("wide", None),
        ),
        out_specs=(
            P("wide", None, "rows", None, None),
            P("wide", None, "rows", None, None),
            P("wide", None),
            P("wide", None),
        ),
        check_vma=False,
    )
```

```python
import functools
import math


import jax
import jax.numpy as jnp
from jax import lax
from jax.experimental import pallas as pl
from jax.experimental.pallas import tpu as pltpu
from jax.sharding import PartitionSpec as P


def with_halo(block, sides, width):
    for axis, dim in sides:
        count = lax.axis_size(axis)
        forward = [(i, i + 1) for i in range(count - 1)]
        backward = [(target, source) for source, target in forward]
        low = lax.ppermute(
            lax.slice_in_dim(block, block.shape[dim] - width, None, axis=dim), axis, forward
        )
        high = lax.ppermute(lax.slice_in_dim(block, 0, width, axis=dim), axis, backward)
        block = jnp.concatenate([low, block, high], axis=dim)
    return block


def silu_slope(values):
    sig = jax.nn.sigmoid(values)
    return sig * (1.0 + values * (1.0 - sig))


def weight_pieces(w_first, w_second, band_count):
    rows_local, channels = w_first.shape
    part = channels // band_count
    me = lax.axis_index("rows")
    both = jnp.stack([w_first, w_second])
    mine = lax.dynamic_slice_in_dim(both, me * part, part, axis=2)
    return jnp.transpose(mine, (0, 2, 1)).reshape(2 * part * rows_local)


def assemble_weights(pieces, band_count, rows_local, channels):
    count = pieces.shape[0]
    part = channels // band_count
    block = pieces.reshape(count, 2, part, rows_local)
    block = jnp.transpose(block, (1, 2, 0, 3)).reshape(2, part, count * rows_local)
    full = lax.all_gather(block, "rows", axis=1, tiled=True)
    return full[0], full[1]


def _wide_sum_kernel(outer, inner, x_ref, o_ref, recv1, part, recv2, send1, got1, send2, got2):
    me = lax.axis_index("wide")
    band = lax.axis_index("rows")
    my_o = me // inner
    my_i = lax.rem(me, inner)
    mesh_id = pl.DeviceIdType.MESH
    barrier = pltpu.get_barrier_semaphore()

    def greet_inner(k, carry):
        peer = my_o * inner + lax.rem(my_i + k, inner)
        pl.semaphore_signal(barrier, 1, device_id=(peer, band), device_id_type=mesh_id)
        return carry

    def greet_outer(k, carry):
        peer = lax.rem(my_o + k, outer) * inner + my_i
        pl.semaphore_signal(barrier, 1, device_id=(peer, band), device_id_type=mesh_id)
        return carry

    lax.fori_loop(1, inner, greet_inner, 0)
    lax.fori_loop(1, outer, greet_outer, 0)
    pl.semaphore_wait(barrier, inner + outer - 2)

    def first_copy(peer_i, slot):
        return pltpu.make_async_remote_copy(
            src_ref=x_ref.at[peer_i],
            dst_ref=recv1.at[slot],
            send_sem=send1.at[peer_i],
            recv_sem=got1.at[slot],
            device_id=(my_o * inner + peer_i, band),
            device_id_type=mesh_id,
        )

    def send_first(k, carry):
        first_copy(lax.rem(my_i + k, inner), my_i).start()
        return carry

    lax.fori_loop(1, inner, send_first, 0)

    def finish_first(k, total):
        first_copy(lax.rem(my_i + k, inner), my_i).wait_send()
        source = lax.rem(my_i + inner - k, inner)
        first_copy(source, source).wait_recv()
        return total + recv1[source]

    part[...] = lax.fori_loop(1, inner, finish_first, x_ref[my_i])

    def second_copy(peer_o, slot):
        return pltpu.make_async_remote_copy(
            src_ref=part.at[peer_o],
            dst_ref=recv2.at[slot],
            send_sem=send2.at[peer_o],
            recv_sem=got2.at[slot],
            device_id=(peer_o * inner + my_i, band),
            device_id_type=mesh_id,
        )

    def send_second(k, carry):
        second_copy(lax.rem(my_o + k, outer), my_o).start()
        return carry

    lax.fori_loop(1, outer, send_second, 0)

    def finish_second(k, total):
        second_copy(lax.rem(my_o + k, outer), my_o).wait_send()
        source = lax.rem(my_o + outer - k, outer)
        second_copy(source, source).wait_recv()
        return total + recv2[source]

    o_ref[...] = lax.fori_loop(1, outer, finish_second, part[my_o])


def wide_sum(pieces):
    count, tall, lanes = pieces.shape
    inner = 8 if count % 8 == 0 else 1
    outer = count // inner
    arranged = jnp.transpose(pieces.reshape(outer, inner, tall, lanes), (1, 0, 2, 3))
    return pl.pallas_call(
        functools.partial(_wide_sum_kernel, outer, inner),
        out_shape=jax.ShapeDtypeStruct((tall, lanes), pieces.dtype),
        in_specs=[pl.BlockSpec(memory_space=pltpu.VMEM)],
        out_specs=pl.BlockSpec(memory_space=pltpu.VMEM),
        scratch_shapes=[
            pltpu.VMEM((inner, outer, tall, lanes), pieces.dtype),
            pltpu.VMEM((outer, tall, lanes), pieces.dtype),
            pltpu.VMEM((outer, tall, lanes), pieces.dtype),
            pltpu.SemaphoreType.DMA((inner,)),
            pltpu.SemaphoreType.DMA((inner,)),
            pltpu.SemaphoreType.DMA((outer,)),
            pltpu.SemaphoreType.DMA((outer,)),
        ],
        compiler_params=pltpu.CompilerParams(collective_id=0, has_side_effects=True),
    )(arranged)


def reduce_weight_grads(grad_t, band_count, wide_size):
    _, channels, total_rows = grad_t.shape
    part = channels // band_count
    chunk = total_rows // wide_size
    blocks = grad_t.astype(jnp.bfloat16).reshape(2, band_count, part, total_rows)
    blocks = jnp.transpose(blocks, (1, 0, 2, 3))
    band_parts = lax.all_to_all(blocks, "rows", 0, 0, tiled=True)
    band_sum = jnp.sum(band_parts.astype(jnp.float32), axis=0)
    band_sum = band_sum.reshape(2, part, wide_size, chunk)
    band_sum = jnp.transpose(band_sum, (2, 0, 1, 3)).reshape(wide_size, 2 * part * chunk)
    size = band_sum.shape[1]
    lanes = 128
    tall = -(-size // (8 * lanes)) * 8
    padded = jnp.pad(band_sum, ((0, 0), (0, tall * lanes - size)))
    share = wide_sum(padded.reshape(wide_size, tall, lanes)).reshape(1, tall * lanes)[:, :size]
    joined = lax.all_to_all(
        jnp.broadcast_to(share, (band_count,) + share.shape[1:]), "rows", 0, 0, tiled=True
    )
    joined = joined.reshape(band_count, 2, part, chunk)
    joined = jnp.transpose(joined, (1, 3, 0, 2)).reshape(2, chunk, channels)
    return joined[0], joined[1]


def conv_forward_t(extended, kernel_t):
    cout = kernel_t.shape[0]
    kernel = kernel_t.reshape(cout, 3, 3, 3, -1)
    padded = jnp.concatenate([extended[:1], extended[:1], extended], axis=0)
    result = lax.conv_general_dilated(
        padded[None], kernel, (1, 1, 1), ((0, 0), (0, 0), (1, 1)),
        dimension_numbers=("NDHWC", "ODHWI", "NDHWC"), preferred_element_type=jnp.float32,
    )
    return result[0]


def conv_weight_grad_t(extended, upstream):
    padded = jnp.concatenate([extended[:1], extended[:1], extended], axis=0)
    result = lax.conv_general_dilated(
        padded[None], upstream[None], (1, 1, 1), ((0, 0), (0, 0), (1, 1)),
        dimension_numbers=("CDHWN", "IDHWO", "CDHWN"), preferred_element_type=jnp.float32,
    )
    return result.reshape(upstream.shape[-1], -1)


def conv_data_grad_t(upstream_ext, kernel_t):
    cout = kernel_t.shape[0]
    kernel = kernel_t.reshape(cout, 3, 3, 3, -1)[:, ::-1, ::-1, ::-1, :]
    padded = jnp.pad(upstream_ext, ((2, 2), (0, 0), (0, 0), (0, 0)))
    result = lax.conv_general_dilated(
        padded[None], kernel, (1, 1, 1), ((0, 0), (0, 0), (1, 1)),
        dimension_numbers=("NDHWC", "IDHWO", "NDHWC"), preferred_element_type=jnp.float32,
    )[0]
    head = (result[0] + result[1] + result[2])[None]
    return jnp.concatenate([head, result[3:]], axis=0)


def body(slabs, dest, pos, lengths, cot, w_first, w_second):
    wide_size = lax.axis_size("wide")
    band_count = lax.axis_size("rows")
    slab_count = slabs.shape[2]
    columns = slabs.shape[3]
    channels = slabs.shape[4]
    frames = cot.shape[1]
    band_rows = cot.shape[2]
    rows_local = w_first.shape[0]
    capacity = -(-slab_count // wide_size)
    slot_count = wide_size * capacity
    targets = dest[0, 0]
    places = pos[0, 0]
    ranking = jnp.arange(slab_count, dtype=jnp.int32)
    earlier = (targets[None, :] == targets[:, None]) & (ranking[None, :] < ranking[:, None])
    slab_rank = jnp.sum(earlier.astype(jnp.int32), axis=1)
    slot_of = targets * capacity + slab_rank
    placing = slot_of[None, :] == jnp.arange(slot_count, dtype=jnp.int32)[:, None]
    flat_slabs = slabs[0, 0].reshape(slab_count, columns * channels)
    outgoing = jnp.dot(placing.astype(jnp.bfloat16), flat_slabs, preferred_element_type=jnp.float32)
    outgoing = outgoing.astype(jnp.bfloat16).reshape(wide_size, capacity * columns * channels)
    labels = jnp.sum(jnp.where(placing, places[None, :] + 1, 0), axis=1) - 1
    labels = labels.reshape(wide_size, capacity).astype(jnp.bfloat16)
    label_block = 128
    pieces = weight_pieces(w_first, w_second, band_count)
    pieces = lax.all_to_all(
        jnp.broadcast_to(pieces[None], (wide_size, pieces.shape[0])), "wide", 0, 0, tiled=True
    )
    kernel_first, kernel_second = assemble_weights(pieces, band_count, rows_local, channels)
    tagged = jnp.concatenate(
        [outgoing, jnp.repeat(labels, label_block // capacity, axis=1)], axis=1
    )
    tagged = lax.all_to_all(tagged, "wide", split_axis=0, concat_axis=0, tiled=True)
    payload = capacity * columns * channels
    arrived = tagged[:, :payload].reshape(slot_count, columns * channels)
    arrived_places = tagged[:, payload : payload + label_block : label_block // capacity]
    arrived_places = arrived_places.astype(jnp.int32).reshape(slot_count)
    settle = arrived_places[None, :] == jnp.arange(slab_count, dtype=jnp.int32)[:, None]
    tile = jnp.dot(settle.astype(jnp.bfloat16), arrived, preferred_element_type=jnp.float32)
    tile = tile.astype(jnp.bfloat16).reshape(frames, band_rows, columns, channels)
    tile_wide = tile.astype(jnp.float32)
    first = jax.nn.silu(tile_wide).astype(jnp.bfloat16)
    first_ext = with_halo(first, (("rows", 1),), 1)
    act = conv_forward_t(first_ext, kernel_first).astype(jnp.bfloat16)
    second = jax.nn.silu(act.astype(jnp.float32)).astype(jnp.bfloat16)
    second_ext = with_halo(second, (("rows", 1),), 1)
    block_out = (tile_wide + conv_forward_t(second_ext, kernel_second)).astype(jnp.bfloat16)
    live = (jnp.arange(frames, dtype=jnp.int32) < lengths[0])[:, None, None, None]
    out_grad = jnp.where(live, cot[0], jnp.zeros_like(cot[0]))
    out_grad_ext = with_halo(out_grad, (("rows", 1),), 1)
    weight_second = conv_weight_grad_t(second_ext, out_grad)
    hidden_grad = conv_data_grad_t(out_grad_ext, kernel_second)
    act_grad = (hidden_grad * silu_slope(act.astype(jnp.float32))).astype(jnp.bfloat16)
    act_grad_ext = with_halo(act_grad, (("rows", 1),), 1)
    weight_first = conv_weight_grad_t(first_ext, act_grad)
    first_grad = conv_data_grad_t(act_grad_ext, kernel_first)
    grad_input = (out_grad.astype(jnp.float32) + first_grad * silu_slope(tile_wide)).astype(
        jnp.bfloat16
    )
    scale = 1.0 / math.sqrt(frames * band_rows * columns * band_count * wide_size)
    grads = jnp.stack([weight_first, weight_second]) * scale
    share_first, share_second = reduce_weight_grads(grads, band_count, wide_size)
    return (block_out[None], grad_input[None], share_first, share_second)


def solution(mesh):

    return jax.shard_map(
        body,
        mesh=mesh,
        in_specs=(
            P("wide", "rows", None, None, None),
            P("wide", "rows", None),
            P("wide", "rows", None),
            P("wide"),
            P("wide", None, "rows", None, None),
            P("wide", None),
            P("wide", None),
        ),
        out_specs=(
            P("wide", None, "rows", None, None),
            P("wide", None, "rows", None, None),
            P("wide", None),
            P("wide", None),
        ),
        check_vma=False,
    )
```

```python
import functools
import math


import jax
import jax.numpy as jnp
from jax import lax
from jax.experimental import pallas as pl
from jax.experimental.pallas import tpu as pltpu
from jax.sharding import PartitionSpec as P


def with_halo(block, sides, width):
    for axis, dim in sides:
        count = lax.axis_size(axis)
        forward = [(i, i + 1) for i in range(count - 1)]
        backward = [(target, source) for source, target in forward]
        low = lax.ppermute(
            lax.slice_in_dim(block, block.shape[dim] - width, None, axis=dim), axis, forward
        )
        high = lax.ppermute(lax.slice_in_dim(block, 0, width, axis=dim), axis, backward)
        block = jnp.concatenate([low, block, high], axis=dim)
    return block


def silu_slope(values):
    sig = jax.nn.sigmoid(values)
    return sig * (1.0 + values * (1.0 - sig))


def weight_pieces(w_first, w_second, band_count):
    rows_local, channels = w_first.shape
    part = channels // band_count
    me = lax.axis_index("rows")
    both = jnp.stack([w_first, w_second])
    mine = lax.dynamic_slice_in_dim(both, me * part, part, axis=2)
    return jnp.transpose(mine, (0, 2, 1)).reshape(2 * part * rows_local)


def assemble_weights(pieces, band_count, rows_local, channels):
    count = pieces.shape[0]
    part = channels // band_count
    block = pieces.reshape(count, 2, part, rows_local)
    block = jnp.transpose(block, (1, 2, 0, 3)).reshape(2, part, count * rows_local)
    full = lax.all_gather(block, "rows", axis=1, tiled=True)
    return full[0], full[1]


def _wide_sum_kernel(outer, inner, x_ref, o_ref, recv1, part, recv2, send1, got1, send2, got2):
    me = lax.axis_index("wide")
    band = lax.axis_index("rows")
    my_o = me // inner
    my_i = lax.rem(me, inner)
    mesh_id = pl.DeviceIdType.MESH
    barrier = pltpu.get_barrier_semaphore()

    def greet_inner(k, carry):
        peer = my_o * inner + lax.rem(my_i + k, inner)
        pl.semaphore_signal(barrier, 1, device_id=(peer, band), device_id_type=mesh_id)
        return carry

    def greet_outer(k, carry):
        peer = lax.rem(my_o + k, outer) * inner + my_i
        pl.semaphore_signal(barrier, 1, device_id=(peer, band), device_id_type=mesh_id)
        return carry

    lax.fori_loop(1, inner, greet_inner, 0)
    lax.fori_loop(1, outer, greet_outer, 0)
    pl.semaphore_wait(barrier, inner + outer - 2)

    def first_copy(peer_i, slot):
        return pltpu.make_async_remote_copy(
            src_ref=x_ref.at[peer_i],
            dst_ref=recv1.at[slot],
            send_sem=send1.at[peer_i],
            recv_sem=got1.at[slot],
            device_id=(my_o * inner + peer_i, band),
            device_id_type=mesh_id,
        )

    def send_first(k, carry):
        first_copy(lax.rem(my_i + k, inner), my_i).start()
        return carry

    lax.fori_loop(1, inner, send_first, 0)

    def finish_first(k, total):
        first_copy(lax.rem(my_i + k, inner), my_i).wait_send()
        source = lax.rem(my_i + inner - k, inner)
        first_copy(source, source).wait_recv()
        return total + recv1[source]

    part[...] = lax.fori_loop(1, inner, finish_first, x_ref[my_i])

    def second_copy(peer_o, slot):
        return pltpu.make_async_remote_copy(
            src_ref=part.at[peer_o],
            dst_ref=recv2.at[slot],
            send_sem=send2.at[peer_o],
            recv_sem=got2.at[slot],
            device_id=(peer_o * inner + my_i, band),
            device_id_type=mesh_id,
        )

    def send_second(k, carry):
        second_copy(lax.rem(my_o + k, outer), my_o).start()
        return carry

    lax.fori_loop(1, outer, send_second, 0)

    def finish_second(k, total):
        second_copy(lax.rem(my_o + k, outer), my_o).wait_send()
        source = lax.rem(my_o + outer - k, outer)
        second_copy(source, source).wait_recv()
        return total + recv2[source]

    o_ref[...] = lax.fori_loop(1, outer, finish_second, part[my_o])


def wide_sum(pieces):
    count, tall, lanes = pieces.shape
    inner = 8 if count % 8 == 0 else 1
    outer = count // inner
    arranged = jnp.transpose(pieces.reshape(outer, inner, tall, lanes), (1, 0, 2, 3))
    return pl.pallas_call(
        functools.partial(_wide_sum_kernel, outer, inner),
        out_shape=jax.ShapeDtypeStruct((tall, lanes), pieces.dtype),
        in_specs=[pl.BlockSpec(memory_space=pltpu.VMEM)],
        out_specs=pl.BlockSpec(memory_space=pltpu.VMEM),
        scratch_shapes=[
            pltpu.VMEM((inner, outer, tall, lanes), pieces.dtype),
            pltpu.VMEM((outer, tall, lanes), pieces.dtype),
            pltpu.VMEM((outer, tall, lanes), pieces.dtype),
            pltpu.SemaphoreType.DMA((inner,)),
            pltpu.SemaphoreType.DMA((inner,)),
            pltpu.SemaphoreType.DMA((outer,)),
            pltpu.SemaphoreType.DMA((outer,)),
        ],
        compiler_params=pltpu.CompilerParams(collective_id=0, has_side_effects=True),
    )(arranged)


def rows_reduce(blocks, band_count):
    me = lax.axis_index("rows")
    core = lax.rem(me, 2)
    chip = me // 2
    chips = band_count // 2
    pairs = blocks.reshape((chips, 2) + blocks.shape[1:])
    keep = lax.dynamic_index_in_dim(pairs, core, axis=1, keepdims=False)
    give = lax.dynamic_index_in_dim(pairs, 1 - core, axis=1, keepdims=False)
    partner = [(r, r + 1 - 2 * (r % 2)) for r in range(band_count)]
    got = lax.ppermute(give, "rows", partner)
    mine = keep.astype(jnp.float32) + got.astype(jnp.float32)
    outgoing = mine.astype(jnp.bfloat16)
    total = lax.dynamic_index_in_dim(mine, chip, axis=0, keepdims=False)
    for shift in range(1, chips):
        route = [(r, ((r // 2 + shift) % chips) * 2 + r % 2) for r in range(band_count)]
        piece = lax.dynamic_index_in_dim(outgoing, lax.rem(chip + shift, chips), axis=0, keepdims=False)
        total = total + lax.ppermute(piece, "rows", route).astype(jnp.float32)
    return total


def reduce_weight_grads(grad_t, band_count, wide_size):
    _, channels, total_rows = grad_t.shape
    part = channels // band_count
    chunk = total_rows // wide_size
    blocks = grad_t.astype(jnp.bfloat16).reshape(2, band_count, part, total_rows)
    blocks = jnp.transpose(blocks, (1, 0, 2, 3))
    band_sum = rows_reduce(blocks, band_count)
    band_sum = band_sum.reshape(2, part, wide_size, chunk)
    band_sum = jnp.transpose(band_sum, (2, 0, 1, 3)).reshape(wide_size, 2 * part * chunk)
    size = band_sum.shape[1]
    lanes = 128
    tall = -(-size // (8 * lanes)) * 8
    padded = jnp.pad(band_sum, ((0, 0), (0, tall * lanes - size)))
    share = wide_sum(padded.reshape(wide_size, tall, lanes)).reshape(1, tall * lanes)[:, :size]
    joined = lax.all_to_all(
        jnp.broadcast_to(share, (band_count,) + share.shape[1:]), "rows", 0, 0, tiled=True
    )
    joined = joined.reshape(band_count, 2, part, chunk)
    joined = jnp.transpose(joined, (1, 3, 0, 2)).reshape(2, chunk, channels)
    return joined[0], joined[1]


def conv_forward_t(extended, kernel_t):
    cout = kernel_t.shape[0]
    kernel = kernel_t.reshape(cout, 3, 3, 3, -1)
    padded = jnp.concatenate([extended[:1], extended[:1], extended], axis=0)
    result = lax.conv_general_dilated(
        padded[None], kernel, (1, 1, 1), ((0, 0), (0, 0), (1, 1)),
        dimension_numbers=("NDHWC", "ODHWI", "NDHWC"), preferred_element_type=jnp.float32,
    )
    return result[0]


def conv_weight_grad_t(extended, upstream):
    padded = jnp.concatenate([extended[:1], extended[:1], extended], axis=0)
    result = lax.conv_general_dilated(
        padded[None], upstream[None], (1, 1, 1), ((0, 0), (0, 0), (1, 1)),
        dimension_numbers=("CDHWN", "IDHWO", "CDHWN"), preferred_element_type=jnp.float32,
    )
    return result.reshape(upstream.shape[-1], -1)


def conv_data_grad_t(upstream_ext, kernel_t):
    cout = kernel_t.shape[0]
    kernel = kernel_t.reshape(cout, 3, 3, 3, -1)[:, ::-1, ::-1, ::-1, :]
    padded = jnp.pad(upstream_ext, ((2, 2), (0, 0), (0, 0), (0, 0)))
    result = lax.conv_general_dilated(
        padded[None], kernel, (1, 1, 1), ((0, 0), (0, 0), (1, 1)),
        dimension_numbers=("NDHWC", "IDHWO", "NDHWC"), preferred_element_type=jnp.float32,
    )[0]
    head = (result[0] + result[1] + result[2])[None]
    return jnp.concatenate([head, result[3:]], axis=0)


def body(slabs, dest, pos, lengths, cot, w_first, w_second):
    wide_size = lax.axis_size("wide")
    band_count = lax.axis_size("rows")
    slab_count = slabs.shape[2]
    columns = slabs.shape[3]
    channels = slabs.shape[4]
    frames = cot.shape[1]
    band_rows = cot.shape[2]
    rows_local = w_first.shape[0]
    capacity = -(-slab_count // wide_size)
    slot_count = wide_size * capacity
    targets = dest[0, 0]
    places = pos[0, 0]
    ranking = jnp.arange(slab_count, dtype=jnp.int32)
    earlier = (targets[None, :] == targets[:, None]) & (ranking[None, :] < ranking[:, None])
    slab_rank = jnp.sum(earlier.astype(jnp.int32), axis=1)
    slot_of = targets * capacity + slab_rank
    placing = slot_of[None, :] == jnp.arange(slot_count, dtype=jnp.int32)[:, None]
    flat_slabs = slabs[0, 0].reshape(slab_count, columns * channels)
    outgoing = jnp.dot(placing.astype(jnp.bfloat16), flat_slabs, preferred_element_type=jnp.float32)
    outgoing = outgoing.astype(jnp.bfloat16).reshape(wide_size, capacity * columns * channels)
    labels = jnp.sum(jnp.where(placing, places[None, :] + 1, 0), axis=1) - 1
    labels = labels.reshape(wide_size, capacity).astype(jnp.bfloat16)
    label_block = 128
    pieces = weight_pieces(w_first, w_second, band_count)
    pieces = lax.all_to_all(
        jnp.broadcast_to(pieces[None], (wide_size, pieces.shape[0])), "wide", 0, 0, tiled=True
    )
    kernel_first, kernel_second = assemble_weights(pieces, band_count, rows_local, channels)
    tagged = jnp.concatenate(
        [outgoing, jnp.repeat(labels, label_block // capacity, axis=1)], axis=1
    )
    tagged = lax.all_to_all(tagged, "wide", split_axis=0, concat_axis=0, tiled=True)
    payload = capacity * columns * channels
    arrived = tagged[:, :payload].reshape(slot_count, columns * channels)
    arrived_places = tagged[:, payload : payload + label_block : label_block // capacity]
    arrived_places = arrived_places.astype(jnp.int32).reshape(slot_count)
    settle = arrived_places[None, :] == jnp.arange(slab_count, dtype=jnp.int32)[:, None]
    tile = jnp.dot(settle.astype(jnp.bfloat16), arrived, preferred_element_type=jnp.float32)
    tile = tile.astype(jnp.bfloat16).reshape(frames, band_rows, columns, channels)
    tile_wide = tile.astype(jnp.float32)
    first = jax.nn.silu(tile_wide).astype(jnp.bfloat16)
    first_ext = with_halo(first, (("rows", 1),), 1)
    act = conv_forward_t(first_ext, kernel_first).astype(jnp.bfloat16)
    second = jax.nn.silu(act.astype(jnp.float32)).astype(jnp.bfloat16)
    second_ext = with_halo(second, (("rows", 1),), 1)
    block_out = (tile_wide + conv_forward_t(second_ext, kernel_second)).astype(jnp.bfloat16)
    live = (jnp.arange(frames, dtype=jnp.int32) < lengths[0])[:, None, None, None]
    out_grad = jnp.where(live, cot[0], jnp.zeros_like(cot[0]))
    out_grad_ext = with_halo(out_grad, (("rows", 1),), 1)
    weight_second = conv_weight_grad_t(second_ext, out_grad)
    hidden_grad = conv_data_grad_t(out_grad_ext, kernel_second)
    act_grad = (hidden_grad * silu_slope(act.astype(jnp.float32))).astype(jnp.bfloat16)
    act_grad_ext = with_halo(act_grad, (("rows", 1),), 1)
    weight_first = conv_weight_grad_t(first_ext, act_grad)
    first_grad = conv_data_grad_t(act_grad_ext, kernel_first)
    grad_input = (out_grad.astype(jnp.float32) + first_grad * silu_slope(tile_wide)).astype(
        jnp.bfloat16
    )
    scale = 1.0 / math.sqrt(frames * band_rows * columns * band_count * wide_size)
    grads = jnp.stack([weight_first, weight_second]) * scale
    share_first, share_second = reduce_weight_grads(grads, band_count, wide_size)
    return (block_out[None], grad_input[None], share_first, share_second)


def solution(mesh):

    return jax.shard_map(
        body,
        mesh=mesh,
        in_specs=(
            P("wide", "rows", None, None, None),
            P("wide", "rows", None),
            P("wide", "rows", None),
            P("wide"),
            P("wide", None, "rows", None, None),
            P("wide", None),
            P("wide", None),
        ),
        out_specs=(
            P("wide", None, "rows", None, None),
            P("wide", None, "rows", None, None),
            P("wide", None),
            P("wide", None),
        ),
        check_vma=False,
    )
```

```python
import functools
import math


import jax
import jax.numpy as jnp
from jax import lax
from jax.experimental import pallas as pl
from jax.experimental.pallas import tpu as pltpu
from jax.sharding import PartitionSpec as P


def with_halo(block, sides, width):
    for axis, dim in sides:
        count = lax.axis_size(axis)
        forward = [(i, i + 1) for i in range(count - 1)]
        backward = [(target, source) for source, target in forward]
        low = lax.ppermute(
            lax.slice_in_dim(block, block.shape[dim] - width, None, axis=dim), axis, forward
        )
        high = lax.ppermute(lax.slice_in_dim(block, 0, width, axis=dim), axis, backward)
        block = jnp.concatenate([low, block, high], axis=dim)
    return block


def silu_slope(values):
    sig = jax.nn.sigmoid(values)
    return sig * (1.0 + values * (1.0 - sig))


def weight_pieces(w_first, w_second, band_count):
    rows_local, channels = w_first.shape
    part = channels // band_count
    me = lax.axis_index("rows")
    both = jnp.stack([w_first, w_second])
    mine = lax.dynamic_slice_in_dim(both, me * part, part, axis=2)
    return jnp.transpose(mine, (0, 2, 1)).reshape(2 * part * rows_local)


def assemble_weights(pieces, band_count, rows_local, channels):
    count = pieces.shape[0]
    part = channels // band_count
    block = pieces.reshape(count, 2, part, rows_local)
    block = jnp.transpose(block, (1, 2, 0, 3)).reshape(2, part, count * rows_local)
    full = rows_gather(block, band_count)
    full = jnp.transpose(full, (1, 0, 2, 3)).reshape(2, channels, count * rows_local)
    return full[0], full[1]


def rows_gather(block, band_count):
    me = lax.axis_index("rows")
    core = lax.rem(me, 2)
    chip = me // 2
    chips = band_count // 2
    partner = [(r, r + 1 - 2 * (r % 2)) for r in range(band_count)]
    got = lax.ppermute(block, "rows", partner)
    pair = jnp.where(core == 0, jnp.stack([block, got]), jnp.stack([got, block]))
    held = [pair]
    for shift in range(1, chips):
        route = [(r, ((r // 2 + shift) % chips) * 2 + r % 2) for r in range(band_count)]
        held.append(lax.ppermute(pair, "rows", route))
    order = lax.rem(chip - jnp.arange(chips, dtype=jnp.int32) + chips, chips)
    full = jnp.take(jnp.stack(held), order, axis=0)
    return full.reshape((band_count,) + block.shape)


def _wide_sum_kernel(outer, inner, x_ref, o_ref, recv1, part, recv2, send1, got1, send2, got2):
    me = lax.axis_index("wide")
    band = lax.axis_index("rows")
    my_o = me // inner
    my_i = lax.rem(me, inner)
    mesh_id = pl.DeviceIdType.MESH
    barrier = pltpu.get_barrier_semaphore()

    def greet_inner(k, carry):
        peer = my_o * inner + lax.rem(my_i + k, inner)
        pl.semaphore_signal(barrier, 1, device_id=(peer, band), device_id_type=mesh_id)
        return carry

    def greet_outer(k, carry):
        peer = lax.rem(my_o + k, outer) * inner + my_i
        pl.semaphore_signal(barrier, 1, device_id=(peer, band), device_id_type=mesh_id)
        return carry

    lax.fori_loop(1, inner, greet_inner, 0)
    lax.fori_loop(1, outer, greet_outer, 0)
    pl.semaphore_wait(barrier, inner + outer - 2)

    def first_copy(peer_i, slot):
        return pltpu.make_async_remote_copy(
            src_ref=x_ref.at[peer_i],
            dst_ref=recv1.at[slot],
            send_sem=send1.at[peer_i],
            recv_sem=got1.at[slot],
            device_id=(my_o * inner + peer_i, band),
            device_id_type=mesh_id,
        )

    def send_first(k, carry):
        first_copy(lax.rem(my_i + k, inner), my_i).start()
        return carry

    lax.fori_loop(1, inner, send_first, 0)

    def finish_first(k, total):
        first_copy(lax.rem(my_i + k, inner), my_i).wait_send()
        source = lax.rem(my_i + inner - k, inner)
        first_copy(source, source).wait_recv()
        return total + recv1[source]

    part[...] = lax.fori_loop(1, inner, finish_first, x_ref[my_i])

    def second_copy(peer_o, slot):
        return pltpu.make_async_remote_copy(
            src_ref=part.at[peer_o],
            dst_ref=recv2.at[slot],
            send_sem=send2.at[peer_o],
            recv_sem=got2.at[slot],
            device_id=(peer_o * inner + my_i, band),
            device_id_type=mesh_id,
        )

    def send_second(k, carry):
        second_copy(lax.rem(my_o + k, outer), my_o).start()
        return carry

    lax.fori_loop(1, outer, send_second, 0)

    def finish_second(k, total):
        second_copy(lax.rem(my_o + k, outer), my_o).wait_send()
        source = lax.rem(my_o + outer - k, outer)
        second_copy(source, source).wait_recv()
        return total + recv2[source]

    o_ref[...] = lax.fori_loop(1, outer, finish_second, part[my_o])


def wide_sum(pieces):
    count, tall, lanes = pieces.shape
    inner = 8 if count % 8 == 0 else 1
    outer = count // inner
    arranged = jnp.transpose(pieces.reshape(outer, inner, tall, lanes), (1, 0, 2, 3))
    return pl.pallas_call(
        functools.partial(_wide_sum_kernel, outer, inner),
        out_shape=jax.ShapeDtypeStruct((tall, lanes), pieces.dtype),
        in_specs=[pl.BlockSpec(memory_space=pltpu.VMEM)],
        out_specs=pl.BlockSpec(memory_space=pltpu.VMEM),
        scratch_shapes=[
            pltpu.VMEM((inner, outer, tall, lanes), pieces.dtype),
            pltpu.VMEM((outer, tall, lanes), pieces.dtype),
            pltpu.VMEM((outer, tall, lanes), pieces.dtype),
            pltpu.SemaphoreType.DMA((inner,)),
            pltpu.SemaphoreType.DMA((inner,)),
            pltpu.SemaphoreType.DMA((outer,)),
            pltpu.SemaphoreType.DMA((outer,)),
        ],
        compiler_params=pltpu.CompilerParams(collective_id=0, has_side_effects=True),
    )(arranged)


def rows_reduce(blocks, band_count):
    me = lax.axis_index("rows")
    core = lax.rem(me, 2)
    chip = me // 2
    chips = band_count // 2
    pairs = blocks.reshape((chips, 2) + blocks.shape[1:])
    keep = lax.dynamic_index_in_dim(pairs, core, axis=1, keepdims=False)
    give = lax.dynamic_index_in_dim(pairs, 1 - core, axis=1, keepdims=False)
    partner = [(r, r + 1 - 2 * (r % 2)) for r in range(band_count)]
    got = lax.ppermute(give, "rows", partner)
    mine = keep.astype(jnp.float32) + got.astype(jnp.float32)
    outgoing = mine.astype(jnp.bfloat16)
    total = lax.dynamic_index_in_dim(mine, chip, axis=0, keepdims=False)
    for shift in range(1, chips):
        route = [(r, ((r // 2 + shift) % chips) * 2 + r % 2) for r in range(band_count)]
        piece = lax.dynamic_index_in_dim(outgoing, lax.rem(chip + shift, chips), axis=0, keepdims=False)
        total = total + lax.ppermute(piece, "rows", route).astype(jnp.float32)
    return total


def reduce_weight_grads(grad_t, band_count, wide_size):
    _, channels, total_rows = grad_t.shape
    part = channels // band_count
    chunk = total_rows // wide_size
    blocks = grad_t.astype(jnp.bfloat16).reshape(2, band_count, part, total_rows)
    blocks = jnp.transpose(blocks, (1, 0, 2, 3))
    band_sum = rows_reduce(blocks, band_count)
    band_sum = band_sum.reshape(2, part, wide_size, chunk)
    band_sum = jnp.transpose(band_sum, (2, 0, 1, 3)).reshape(wide_size, 2 * part * chunk)
    size = band_sum.shape[1]
    lanes = 128
    tall = -(-size // (8 * lanes)) * 8
    padded = jnp.pad(band_sum, ((0, 0), (0, tall * lanes - size)))
    share = wide_sum(padded.reshape(wide_size, tall, lanes)).reshape(1, tall * lanes)[:, :size]
    joined = lax.all_to_all(
        jnp.broadcast_to(share, (band_count,) + share.shape[1:]), "rows", 0, 0, tiled=True
    )
    joined = joined.reshape(band_count, 2, part, chunk)
    joined = jnp.transpose(joined, (1, 3, 0, 2)).reshape(2, chunk, channels)
    return joined[0], joined[1]


def conv_forward_t(extended, kernel_t):
    cout = kernel_t.shape[0]
    kernel = kernel_t.reshape(cout, 3, 3, 3, -1)
    padded = jnp.concatenate([extended[:1], extended[:1], extended], axis=0)
    result = lax.conv_general_dilated(
        padded[None], kernel, (1, 1, 1), ((0, 0), (0, 0), (1, 1)),
        dimension_numbers=("NDHWC", "ODHWI", "NDHWC"), preferred_element_type=jnp.float32,
    )
    return result[0]


def conv_weight_grad_t(extended, upstream):
    padded = jnp.concatenate([extended[:1], extended[:1], extended], axis=0)
    result = lax.conv_general_dilated(
        padded[None], upstream[None], (1, 1, 1), ((0, 0), (0, 0), (1, 1)),
        dimension_numbers=("CDHWN", "IDHWO", "CDHWN"), preferred_element_type=jnp.float32,
    )
    return result.reshape(upstream.shape[-1], -1)


def conv_data_grad_t(upstream_ext, kernel_t):
    cout = kernel_t.shape[0]
    kernel = kernel_t.reshape(cout, 3, 3, 3, -1)[:, ::-1, ::-1, ::-1, :]
    padded = jnp.pad(upstream_ext, ((2, 2), (0, 0), (0, 0), (0, 0)))
    result = lax.conv_general_dilated(
        padded[None], kernel, (1, 1, 1), ((0, 0), (0, 0), (1, 1)),
        dimension_numbers=("NDHWC", "IDHWO", "NDHWC"), preferred_element_type=jnp.float32,
    )[0]
    head = (result[0] + result[1] + result[2])[None]
    return jnp.concatenate([head, result[3:]], axis=0)


def body(slabs, dest, pos, lengths, cot, w_first, w_second):
    wide_size = lax.axis_size("wide")
    band_count = lax.axis_size("rows")
    slab_count = slabs.shape[2]
    columns = slabs.shape[3]
    channels = slabs.shape[4]
    frames = cot.shape[1]
    band_rows = cot.shape[2]
    rows_local = w_first.shape[0]
    capacity = -(-slab_count // wide_size)
    slot_count = wide_size * capacity
    targets = dest[0, 0]
    places = pos[0, 0]
    ranking = jnp.arange(slab_count, dtype=jnp.int32)
    earlier = (targets[None, :] == targets[:, None]) & (ranking[None, :] < ranking[:, None])
    slab_rank = jnp.sum(earlier.astype(jnp.int32), axis=1)
    slot_of = targets * capacity + slab_rank
    placing = slot_of[None, :] == jnp.arange(slot_count, dtype=jnp.int32)[:, None]
    flat_slabs = slabs[0, 0].reshape(slab_count, columns * channels)
    outgoing = jnp.dot(placing.astype(jnp.bfloat16), flat_slabs, preferred_element_type=jnp.float32)
    outgoing = outgoing.astype(jnp.bfloat16).reshape(wide_size, capacity * columns * channels)
    labels = jnp.sum(jnp.where(placing, places[None, :] + 1, 0), axis=1) - 1
    labels = labels.reshape(wide_size, capacity).astype(jnp.bfloat16)
    label_block = 128
    pieces = weight_pieces(w_first, w_second, band_count)
    tagged = jnp.concatenate(
        [
            outgoing,
            jnp.repeat(labels, label_block // capacity, axis=1),
            jnp.broadcast_to(pieces[None], (wide_size, pieces.shape[0])),
        ],
        axis=1,
    )
    tagged = lax.all_to_all(tagged, "wide", split_axis=0, concat_axis=0, tiled=True)
    payload = capacity * columns * channels
    arrived = tagged[:, :payload].reshape(slot_count, columns * channels)
    arrived_places = tagged[:, payload : payload + label_block : label_block // capacity]
    arrived_places = arrived_places.astype(jnp.int32).reshape(slot_count)
    kernel_first, kernel_second = assemble_weights(
        tagged[:, payload + label_block :], band_count, rows_local, channels
    )
    settle = arrived_places[None, :] == jnp.arange(slab_count, dtype=jnp.int32)[:, None]
    tile = jnp.dot(settle.astype(jnp.bfloat16), arrived, preferred_element_type=jnp.float32)
    tile = tile.astype(jnp.bfloat16).reshape(frames, band_rows, columns, channels)
    tile_wide = tile.astype(jnp.float32)
    first = jax.nn.silu(tile_wide).astype(jnp.bfloat16)
    first_ext = with_halo(first, (("rows", 1),), 1)
    act = conv_forward_t(first_ext, kernel_first).astype(jnp.bfloat16)
    second = jax.nn.silu(act.astype(jnp.float32)).astype(jnp.bfloat16)
    second_ext = with_halo(second, (("rows", 1),), 1)
    block_out = (tile_wide + conv_forward_t(second_ext, kernel_second)).astype(jnp.bfloat16)
    live = (jnp.arange(frames, dtype=jnp.int32) < lengths[0])[:, None, None, None]
    out_grad = jnp.where(live, cot[0], jnp.zeros_like(cot[0]))
    out_grad_ext = with_halo(out_grad, (("rows", 1),), 1)
    weight_second = conv_weight_grad_t(second_ext, out_grad)
    hidden_grad = conv_data_grad_t(out_grad_ext, kernel_second)
    act_grad = (hidden_grad * silu_slope(act.astype(jnp.float32))).astype(jnp.bfloat16)
    act_grad_ext = with_halo(act_grad, (("rows", 1),), 1)
    weight_first = conv_weight_grad_t(first_ext, act_grad)
    first_grad = conv_data_grad_t(act_grad_ext, kernel_first)
    grad_input = (out_grad.astype(jnp.float32) + first_grad * silu_slope(tile_wide)).astype(
        jnp.bfloat16
    )
    scale = 1.0 / math.sqrt(frames * band_rows * columns * band_count * wide_size)
    grads = jnp.stack([weight_first, weight_second]) * scale
    share_first, share_second = reduce_weight_grads(grads, band_count, wide_size)
    return (block_out[None], grad_input[None], share_first, share_second)


def solution(mesh):

    return jax.shard_map(
        body,
        mesh=mesh,
        in_specs=(
            P("wide", "rows", None, None, None),
            P("wide", "rows", None),
            P("wide", "rows", None),
            P("wide"),
            P("wide", None, "rows", None, None),
            P("wide", None),
            P("wide", None),
        ),
        out_specs=(
            P("wide", None, "rows", None, None),
            P("wide", None, "rows", None, None),
            P("wide", None),
            P("wide", None),
        ),
        check_vma=False,
    )
```

```python
import functools
import math


import jax
import jax.numpy as jnp
from jax import lax
from jax.experimental import pallas as pl
from jax.experimental.pallas import tpu as pltpu
from jax.sharding import PartitionSpec as P


def with_halo(block, sides, width):
    for axis, dim in sides:
        count = lax.axis_size(axis)
        forward = [(i, i + 1) for i in range(count - 1)]
        backward = [(target, source) for source, target in forward]
        low = lax.ppermute(
            lax.slice_in_dim(block, block.shape[dim] - width, None, axis=dim), axis, forward
        )
        high = lax.ppermute(lax.slice_in_dim(block, 0, width, axis=dim), axis, backward)
        block = jnp.concatenate([low, block, high], axis=dim)
    return block


def silu_slope(values):
    sig = jax.nn.sigmoid(values)
    return sig * (1.0 + values * (1.0 - sig))


def weight_pieces(w_first, w_second, band_count):
    rows_local, channels = w_first.shape
    part = channels // band_count
    me = lax.axis_index("rows")
    both = jnp.stack([w_first, w_second])
    mine = lax.dynamic_slice_in_dim(both, me * part, part, axis=2)
    return jnp.transpose(mine, (0, 2, 1)).reshape(2 * part * rows_local)


def assemble_weights(pieces, band_count, rows_local, channels):
    count = pieces.shape[0]
    part = channels // band_count
    block = pieces.reshape(count, 2, part, rows_local)
    block = jnp.transpose(block, (1, 2, 0, 3)).reshape(2, part, count * rows_local)
    full = rows_gather(block, band_count)
    full = jnp.transpose(full, (1, 0, 2, 3)).reshape(2, channels, count * rows_local)
    return full[0], full[1]


def rows_gather(block, band_count):
    me = lax.axis_index("rows")
    core = lax.rem(me, 2)
    chip = me // 2
    chips = band_count // 2
    partner = [(r, r + 1 - 2 * (r % 2)) for r in range(band_count)]
    got = lax.ppermute(block, "rows", partner)
    pair = jnp.where(core == 0, jnp.stack([block, got]), jnp.stack([got, block]))
    held = [pair]
    for shift in range(1, chips):
        route = [(r, ((r // 2 + shift) % chips) * 2 + r % 2) for r in range(band_count)]
        held.append(lax.ppermute(pair, "rows", route))
    order = lax.rem(chip - jnp.arange(chips, dtype=jnp.int32) + chips, chips)
    full = jnp.take(jnp.stack(held), order, axis=0)
    return full.reshape((band_count,) + block.shape)


def _wide_sum_kernel(outer, inner, x_ref, o_ref, recv1, part, recv2, send1, got1, send2, got2):
    me = lax.axis_index("wide")
    band = lax.axis_index("rows")
    my_o = me // inner
    my_i = lax.rem(me, inner)
    mesh_id = pl.DeviceIdType.MESH
    barrier = pltpu.get_barrier_semaphore()

    def greet_inner(k, carry):
        peer = my_o * inner + lax.rem(my_i + k, inner)
        pl.semaphore_signal(barrier, 1, device_id=(peer, band), device_id_type=mesh_id)
        return carry

    def greet_outer(k, carry):
        peer = lax.rem(my_o + k, outer) * inner + my_i
        pl.semaphore_signal(barrier, 1, device_id=(peer, band), device_id_type=mesh_id)
        return carry

    lax.fori_loop(1, inner, greet_inner, 0)
    lax.fori_loop(1, outer, greet_outer, 0)
    pl.semaphore_wait(barrier, inner + outer - 2)

    def first_copy(peer_i, slot):
        return pltpu.make_async_remote_copy(
            src_ref=x_ref.at[peer_i],
            dst_ref=recv1.at[slot],
            send_sem=send1.at[peer_i],
            recv_sem=got1.at[slot],
            device_id=(my_o * inner + peer_i, band),
            device_id_type=mesh_id,
        )

    def send_first(k, carry):
        first_copy(lax.rem(my_i + k, inner), my_i).start()
        return carry

    lax.fori_loop(1, inner, send_first, 0)

    def finish_first(k, total):
        first_copy(lax.rem(my_i + k, inner), my_i).wait_send()
        source = lax.rem(my_i + inner - k, inner)
        first_copy(source, source).wait_recv()
        return total + recv1[source]

    part[...] = lax.fori_loop(1, inner, finish_first, x_ref[my_i])

    def second_copy(peer_o, slot):
        return pltpu.make_async_remote_copy(
            src_ref=part.at[peer_o],
            dst_ref=recv2.at[slot],
            send_sem=send2.at[peer_o],
            recv_sem=got2.at[slot],
            device_id=(peer_o * inner + my_i, band),
            device_id_type=mesh_id,
        )

    def send_second(k, carry):
        second_copy(lax.rem(my_o + k, outer), my_o).start()
        return carry

    lax.fori_loop(1, outer, send_second, 0)

    def finish_second(k, total):
        second_copy(lax.rem(my_o + k, outer), my_o).wait_send()
        source = lax.rem(my_o + outer - k, outer)
        second_copy(source, source).wait_recv()
        return total + recv2[source]

    o_ref[...] = lax.fori_loop(1, outer, finish_second, part[my_o])


def wide_sum(pieces):
    count, tall, lanes = pieces.shape
    inner = 8 if count % 8 == 0 else 1
    outer = count // inner
    arranged = jnp.transpose(pieces.reshape(outer, inner, tall, lanes), (1, 0, 2, 3))
    return pl.pallas_call(
        functools.partial(_wide_sum_kernel, outer, inner),
        out_shape=jax.ShapeDtypeStruct((tall, lanes), pieces.dtype),
        in_specs=[pl.BlockSpec(memory_space=pltpu.VMEM)],
        out_specs=pl.BlockSpec(memory_space=pltpu.VMEM),
        scratch_shapes=[
            pltpu.VMEM((inner, outer, tall, lanes), pieces.dtype),
            pltpu.VMEM((outer, tall, lanes), pieces.dtype),
            pltpu.VMEM((outer, tall, lanes), pieces.dtype),
            pltpu.SemaphoreType.DMA((inner,)),
            pltpu.SemaphoreType.DMA((inner,)),
            pltpu.SemaphoreType.DMA((outer,)),
            pltpu.SemaphoreType.DMA((outer,)),
        ],
        compiler_params=pltpu.CompilerParams(collective_id=0, has_side_effects=True),
    )(arranged)


def rows_reduce(blocks, band_count):
    me = lax.axis_index("rows")
    core = lax.rem(me, 2)
    chip = me // 2
    chips = band_count // 2
    pairs = blocks.reshape((chips, 2) + blocks.shape[1:])
    keep = lax.dynamic_index_in_dim(pairs, core, axis=1, keepdims=False)
    give = lax.dynamic_index_in_dim(pairs, 1 - core, axis=1, keepdims=False)
    partner = [(r, r + 1 - 2 * (r % 2)) for r in range(band_count)]
    got = lax.ppermute(give, "rows", partner)
    mine = keep.astype(jnp.float32) + got.astype(jnp.float32)
    outgoing = mine.astype(jnp.bfloat16)
    total = lax.dynamic_index_in_dim(mine, chip, axis=0, keepdims=False)
    for shift in range(1, chips):
        route = [(r, ((r // 2 + shift) % chips) * 2 + r % 2) for r in range(band_count)]
        piece = lax.dynamic_index_in_dim(outgoing, lax.rem(chip + shift, chips), axis=0, keepdims=False)
        total = total + lax.ppermute(piece, "rows", route).astype(jnp.float32)
    return total


def reduce_weight_grads(grad_t, band_count, wide_size):
    _, channels, total_rows = grad_t.shape
    part = channels // band_count
    chunk = total_rows // wide_size
    blocks = grad_t.reshape(2, band_count, part, total_rows)
    blocks = jnp.transpose(blocks, (1, 0, 2, 3))
    band_sum = rows_reduce(blocks, band_count)
    band_sum = band_sum.reshape(2, part, wide_size, chunk)
    band_sum = jnp.transpose(band_sum, (2, 0, 1, 3)).reshape(wide_size, 2 * part * chunk)
    size = band_sum.shape[1]
    lanes = 128
    tall = -(-size // (8 * lanes)) * 8
    padded = jnp.pad(band_sum, ((0, 0), (0, tall * lanes - size)))
    share = wide_sum(padded.reshape(wide_size, tall, lanes)).reshape(1, tall * lanes)[:, :size]
    joined = rows_gather(share[0], band_count)
    joined = joined.reshape(band_count, 2, part, chunk)
    joined = jnp.transpose(joined, (1, 3, 0, 2)).reshape(2, chunk, channels)
    return joined[0], joined[1]


def conv_forward_t(extended, kernel_t):
    cout = kernel_t.shape[0]
    kernel = kernel_t.reshape(cout, 3, 3, 3, -1)
    padded = jnp.concatenate([extended[:1], extended[:1], extended], axis=0)
    result = lax.conv_general_dilated(
        padded[None], kernel, (1, 1, 1), ((0, 0), (0, 0), (1, 1)),
        dimension_numbers=("NDHWC", "ODHWI", "NDHWC"), preferred_element_type=jnp.float32,
    )
    return result[0]


def conv_weight_grad_t(extended, upstream):
    padded = jnp.concatenate([extended[:1], extended[:1], extended], axis=0)
    result = lax.conv_general_dilated(
        padded[None], upstream[None], (1, 1, 1), ((0, 0), (0, 0), (1, 1)),
        dimension_numbers=("CDHWN", "IDHWO", "CDHWN"), preferred_element_type=jnp.float32,
    )
    return result.reshape(upstream.shape[-1], -1)


def conv_data_grad_t(upstream_ext, kernel_t):
    cout = kernel_t.shape[0]
    kernel = kernel_t.reshape(cout, 3, 3, 3, -1)[:, ::-1, ::-1, ::-1, :]
    padded = jnp.pad(upstream_ext, ((2, 2), (0, 0), (0, 0), (0, 0)))
    result = lax.conv_general_dilated(
        padded[None], kernel, (1, 1, 1), ((0, 0), (0, 0), (1, 1)),
        dimension_numbers=("NDHWC", "IDHWO", "NDHWC"), preferred_element_type=jnp.float32,
    )[0]
    head = (result[0] + result[1] + result[2])[None]
    return jnp.concatenate([head, result[3:]], axis=0)


def body(slabs, dest, pos, lengths, cot, w_first, w_second):
    wide_size = lax.axis_size("wide")
    band_count = lax.axis_size("rows")
    slab_count = slabs.shape[2]
    columns = slabs.shape[3]
    channels = slabs.shape[4]
    frames = cot.shape[1]
    band_rows = cot.shape[2]
    rows_local = w_first.shape[0]
    capacity = -(-slab_count // wide_size)
    slot_count = wide_size * capacity
    targets = dest[0, 0]
    places = pos[0, 0]
    ranking = jnp.arange(slab_count, dtype=jnp.int32)
    earlier = (targets[None, :] == targets[:, None]) & (ranking[None, :] < ranking[:, None])
    slab_rank = jnp.sum(earlier.astype(jnp.int32), axis=1)
    slot_of = targets * capacity + slab_rank
    placing = slot_of[None, :] == jnp.arange(slot_count, dtype=jnp.int32)[:, None]
    flat_slabs = slabs[0, 0].reshape(slab_count, columns * channels)
    outgoing = jnp.dot(placing.astype(jnp.bfloat16), flat_slabs, preferred_element_type=jnp.float32)
    outgoing = outgoing.astype(jnp.bfloat16).reshape(wide_size, capacity * columns * channels)
    labels = jnp.sum(jnp.where(placing, places[None, :] + 1, 0), axis=1) - 1
    labels = labels.reshape(wide_size, capacity).astype(jnp.bfloat16)
    label_block = 128
    pieces = weight_pieces(w_first, w_second, band_count)
    tagged = jnp.concatenate(
        [
            outgoing,
            jnp.repeat(labels, label_block // capacity, axis=1),
            jnp.broadcast_to(pieces[None], (wide_size, pieces.shape[0])),
        ],
        axis=1,
    )
    tagged = lax.all_to_all(tagged, "wide", split_axis=0, concat_axis=0, tiled=True)
    payload = capacity * columns * channels
    arrived = tagged[:, :payload].reshape(slot_count, columns * channels)
    arrived_places = tagged[:, payload : payload + label_block : label_block // capacity]
    arrived_places = arrived_places.astype(jnp.int32).reshape(slot_count)
    kernel_first, kernel_second = assemble_weights(
        tagged[:, payload + label_block :], band_count, rows_local, channels
    )
    settle = arrived_places[None, :] == jnp.arange(slab_count, dtype=jnp.int32)[:, None]
    tile = jnp.dot(settle.astype(jnp.bfloat16), arrived, preferred_element_type=jnp.float32)
    tile = tile.astype(jnp.bfloat16).reshape(frames, band_rows, columns, channels)
    tile_wide = tile.astype(jnp.float32)
    first = jax.nn.silu(tile_wide).astype(jnp.bfloat16)
    first_ext = with_halo(first, (("rows", 1),), 1)
    act = conv_forward_t(first_ext, kernel_first).astype(jnp.bfloat16)
    second = jax.nn.silu(act.astype(jnp.float32)).astype(jnp.bfloat16)
    second_ext = with_halo(second, (("rows", 1),), 1)
    block_out = (tile_wide + conv_forward_t(second_ext, kernel_second)).astype(jnp.bfloat16)
    live = (jnp.arange(frames, dtype=jnp.int32) < lengths[0])[:, None, None, None]
    out_grad = jnp.where(live, cot[0], jnp.zeros_like(cot[0]))
    out_grad_ext = with_halo(out_grad, (("rows", 1),), 1)
    weight_second = conv_weight_grad_t(second_ext, out_grad)
    hidden_grad = conv_data_grad_t(out_grad_ext, kernel_second)
    act_grad = (hidden_grad * silu_slope(act.astype(jnp.float32))).astype(jnp.bfloat16)
    act_grad_ext = with_halo(act_grad, (("rows", 1),), 1)
    weight_first = conv_weight_grad_t(first_ext, act_grad)
    first_grad = conv_data_grad_t(act_grad_ext, kernel_first)
    grad_input = (out_grad.astype(jnp.float32) + first_grad * silu_slope(tile_wide)).astype(
        jnp.bfloat16
    )
    scale = 1.0 / math.sqrt(frames * band_rows * columns * band_count * wide_size)
    grads = jnp.stack(
        [(weight_first * scale).astype(jnp.bfloat16), (weight_second * scale).astype(jnp.bfloat16)]
    )
    share_first, share_second = reduce_weight_grads(grads, band_count, wide_size)
    return (block_out[None], grad_input[None], share_first, share_second)


def solution(mesh):

    return jax.shard_map(
        body,
        mesh=mesh,
        in_specs=(
            P("wide", "rows", None, None, None),
            P("wide", "rows", None),
            P("wide", "rows", None),
            P("wide"),
            P("wide", None, "rows", None, None),
            P("wide", None),
            P("wide", None),
        ),
        out_specs=(
            P("wide", None, "rows", None, None),
            P("wide", None, "rows", None, None),
            P("wide", None),
            P("wide", None),
        ),
        check_vma=False,
    )
```

```python
import functools
import math


import jax
import jax.numpy as jnp
from jax import lax
from jax.experimental import pallas as pl
from jax.experimental.pallas import tpu as pltpu
from jax.sharding import PartitionSpec as P


def with_halo(block, sides, width):
    for axis, dim in sides:
        count = lax.axis_size(axis)
        forward = [(i, i + 1) for i in range(count - 1)]
        backward = [(target, source) for source, target in forward]
        low = lax.ppermute(
            lax.slice_in_dim(block, block.shape[dim] - width, None, axis=dim), axis, forward
        )
        high = lax.ppermute(lax.slice_in_dim(block, 0, width, axis=dim), axis, backward)
        block = jnp.concatenate([low, block, high], axis=dim)
    return block


def silu_slope(values):
    sig = jax.nn.sigmoid(values)
    return sig * (1.0 + values * (1.0 - sig))


def weight_pieces(w_first, w_second, band_count):
    rows_local, channels = w_first.shape
    part = channels // band_count
    me = lax.axis_index("rows")
    both = jnp.stack([w_first, w_second])
    mine = lax.dynamic_slice_in_dim(both, me * part, part, axis=2)
    return jnp.transpose(mine, (0, 2, 1)).reshape(2 * part * rows_local)


def assemble_weights(pieces, band_count, rows_local, channels):
    count = pieces.shape[0]
    part = channels // band_count
    block = pieces.reshape(count, 2, part, rows_local)
    block = jnp.transpose(block, (1, 2, 0, 3)).reshape(2, part, count * rows_local)
    full = rows_gather(block, band_count)
    full = jnp.transpose(full, (1, 0, 2, 3)).reshape(2, channels, count * rows_local)
    return full[0], full[1]


def rows_gather(block, band_count):
    me = lax.axis_index("rows")
    core = lax.rem(me, 2)
    chip = me // 2
    chips = band_count // 2
    held = [block]
    for shift in range(1, chips):
        route = [(r, ((r // 2 + shift) % chips) * 2 + r % 2) for r in range(band_count)]
        held.append(lax.ppermute(block, "rows", route))
    order = lax.rem(chip - jnp.arange(chips, dtype=jnp.int32) + chips, chips)
    column = jnp.take(jnp.stack(held), order, axis=0)
    partner = [(r, r + 1 - 2 * (r % 2)) for r in range(band_count)]
    got = lax.ppermute(column, "rows", partner)
    full = jnp.where(core == 0, jnp.stack([column, got], axis=1), jnp.stack([got, column], axis=1))
    return full.reshape((band_count,) + block.shape)


def _wide_sum_kernel(outer, inner, x_ref, o_ref, recv1, part, recv2, send1, got1, send2, got2):
    me = lax.axis_index("wide")
    band = lax.axis_index("rows")
    my_o = me // inner
    my_i = lax.rem(me, inner)
    mesh_id = pl.DeviceIdType.MESH
    barrier = pltpu.get_barrier_semaphore()

    def greet_inner(k, carry):
        peer = my_o * inner + lax.rem(my_i + k, inner)
        pl.semaphore_signal(barrier, 1, device_id=(peer, band), device_id_type=mesh_id)
        return carry

    def greet_outer(k, carry):
        peer = lax.rem(my_o + k, outer) * inner + my_i
        pl.semaphore_signal(barrier, 1, device_id=(peer, band), device_id_type=mesh_id)
        return carry

    lax.fori_loop(1, inner, greet_inner, 0)
    lax.fori_loop(1, outer, greet_outer, 0)
    pl.semaphore_wait(barrier, inner + outer - 2)

    def first_copy(peer_i, slot):
        return pltpu.make_async_remote_copy(
            src_ref=x_ref.at[peer_i],
            dst_ref=recv1.at[slot],
            send_sem=send1.at[peer_i],
            recv_sem=got1.at[slot],
            device_id=(my_o * inner + peer_i, band),
            device_id_type=mesh_id,
        )

    def send_first(k, carry):
        first_copy(lax.rem(my_i + k, inner), my_i).start()
        return carry

    lax.fori_loop(1, inner, send_first, 0)

    def finish_first(k, total):
        first_copy(lax.rem(my_i + k, inner), my_i).wait_send()
        source = lax.rem(my_i + inner - k, inner)
        first_copy(source, source).wait_recv()
        return total + recv1[source]

    part[...] = lax.fori_loop(1, inner, finish_first, x_ref[my_i])

    def second_copy(peer_o, slot):
        return pltpu.make_async_remote_copy(
            src_ref=part.at[peer_o],
            dst_ref=recv2.at[slot],
            send_sem=send2.at[peer_o],
            recv_sem=got2.at[slot],
            device_id=(peer_o * inner + my_i, band),
            device_id_type=mesh_id,
        )

    def send_second(k, carry):
        second_copy(lax.rem(my_o + k, outer), my_o).start()
        return carry

    lax.fori_loop(1, outer, send_second, 0)

    def finish_second(k, total):
        second_copy(lax.rem(my_o + k, outer), my_o).wait_send()
        source = lax.rem(my_o + outer - k, outer)
        second_copy(source, source).wait_recv()
        return total + recv2[source]

    o_ref[...] = lax.fori_loop(1, outer, finish_second, part[my_o])


def wide_sum(pieces):
    count, tall, lanes = pieces.shape
    inner = 8 if count % 8 == 0 else 1
    outer = count // inner
    arranged = jnp.transpose(pieces.reshape(outer, inner, tall, lanes), (1, 0, 2, 3))
    return pl.pallas_call(
        functools.partial(_wide_sum_kernel, outer, inner),
        out_shape=jax.ShapeDtypeStruct((tall, lanes), pieces.dtype),
        in_specs=[pl.BlockSpec(memory_space=pltpu.VMEM)],
        out_specs=pl.BlockSpec(memory_space=pltpu.VMEM),
        scratch_shapes=[
            pltpu.VMEM((inner, outer, tall, lanes), pieces.dtype),
            pltpu.VMEM((outer, tall, lanes), pieces.dtype),
            pltpu.VMEM((outer, tall, lanes), pieces.dtype),
            pltpu.SemaphoreType.DMA((inner,)),
            pltpu.SemaphoreType.DMA((inner,)),
            pltpu.SemaphoreType.DMA((outer,)),
            pltpu.SemaphoreType.DMA((outer,)),
        ],
        compiler_params=pltpu.CompilerParams(collective_id=0, has_side_effects=True),
    )(arranged)


def rows_reduce(blocks, band_count):
    me = lax.axis_index("rows")
    core = lax.rem(me, 2)
    chip = me // 2
    chips = band_count // 2
    pairs = blocks.reshape((chips, 2) + blocks.shape[1:])
    keep = lax.dynamic_index_in_dim(pairs, core, axis=1, keepdims=False)
    give = lax.dynamic_index_in_dim(pairs, 1 - core, axis=1, keepdims=False)
    partner = [(r, r + 1 - 2 * (r % 2)) for r in range(band_count)]
    got = lax.ppermute(give, "rows", partner)
    mine = keep.astype(jnp.float32) + got.astype(jnp.float32)
    outgoing = mine.astype(jnp.bfloat16)
    total = lax.dynamic_index_in_dim(mine, chip, axis=0, keepdims=False)
    for shift in range(1, chips):
        route = [(r, ((r // 2 + shift) % chips) * 2 + r % 2) for r in range(band_count)]
        piece = lax.dynamic_index_in_dim(outgoing, lax.rem(chip + shift, chips), axis=0, keepdims=False)
        total = total + lax.ppermute(piece, "rows", route).astype(jnp.float32)
    return total


def reduce_weight_grads(grad_t, band_count, wide_size):
    _, channels, total_rows = grad_t.shape
    part = channels // band_count
    chunk = total_rows // wide_size
    blocks = grad_t.astype(jnp.bfloat16).reshape(2, band_count, part, total_rows)
    blocks = jnp.transpose(blocks, (1, 0, 2, 3))
    band_sum = rows_reduce(blocks, band_count)
    band_sum = band_sum.reshape(2, part, wide_size, chunk)
    band_sum = jnp.transpose(band_sum, (2, 0, 1, 3)).reshape(wide_size, 2 * part * chunk)
    size = band_sum.shape[1]
    lanes = 128
    tall = -(-size // (8 * lanes)) * 8
    padded = jnp.pad(band_sum, ((0, 0), (0, tall * lanes - size)))
    share = wide_sum(padded.reshape(wide_size, tall, lanes)).reshape(1, tall * lanes)[:, :size]
    joined = lax.all_to_all(
        jnp.broadcast_to(share, (band_count,) + share.shape[1:]), "rows", 0, 0, tiled=True
    )
    joined = joined.reshape(band_count, 2, part, chunk)
    joined = jnp.transpose(joined, (1, 3, 0, 2)).reshape(2, chunk, channels)
    return joined[0], joined[1]


def conv_forward_t(extended, kernel_t):
    cout = kernel_t.shape[0]
    kernel = kernel_t.reshape(cout, 3, 3, 3, -1)
    padded = jnp.concatenate([extended[:1], extended[:1], extended], axis=0)
    result = lax.conv_general_dilated(
        padded[None], kernel, (1, 1, 1), ((0, 0), (0, 0), (1, 1)),
        dimension_numbers=("NDHWC", "ODHWI", "NDHWC"), preferred_element_type=jnp.float32,
    )
    return result[0]


def conv_weight_grad_t(extended, upstream):
    padded = jnp.concatenate([extended[:1], extended[:1], extended], axis=0)
    result = lax.conv_general_dilated(
        padded[None], upstream[None], (1, 1, 1), ((0, 0), (0, 0), (1, 1)),
        dimension_numbers=("CDHWN", "IDHWO", "CDHWN"), preferred_element_type=jnp.float32,
    )
    return result.reshape(upstream.shape[-1], -1)


def conv_data_grad_t(upstream_ext, kernel_t):
    cout = kernel_t.shape[0]
    kernel = kernel_t.reshape(cout, 3, 3, 3, -1)[:, ::-1, ::-1, ::-1, :]
    padded = jnp.pad(upstream_ext, ((2, 2), (0, 0), (0, 0), (0, 0)))
    result = lax.conv_general_dilated(
        padded[None], kernel, (1, 1, 1), ((0, 0), (0, 0), (1, 1)),
        dimension_numbers=("NDHWC", "IDHWO", "NDHWC"), preferred_element_type=jnp.float32,
    )[0]
    head = (result[0] + result[1] + result[2])[None]
    return jnp.concatenate([head, result[3:]], axis=0)


def body(slabs, dest, pos, lengths, cot, w_first, w_second):
    wide_size = lax.axis_size("wide")
    band_count = lax.axis_size("rows")
    slab_count = slabs.shape[2]
    columns = slabs.shape[3]
    channels = slabs.shape[4]
    frames = cot.shape[1]
    band_rows = cot.shape[2]
    rows_local = w_first.shape[0]
    capacity = -(-slab_count // wide_size)
    slot_count = wide_size * capacity
    targets = dest[0, 0]
    places = pos[0, 0]
    ranking = jnp.arange(slab_count, dtype=jnp.int32)
    earlier = (targets[None, :] == targets[:, None]) & (ranking[None, :] < ranking[:, None])
    slab_rank = jnp.sum(earlier.astype(jnp.int32), axis=1)
    slot_of = targets * capacity + slab_rank
    placing = slot_of[None, :] == jnp.arange(slot_count, dtype=jnp.int32)[:, None]
    flat_slabs = slabs[0, 0].reshape(slab_count, columns * channels)
    outgoing = jnp.dot(placing.astype(jnp.bfloat16), flat_slabs, preferred_element_type=jnp.float32)
    outgoing = outgoing.astype(jnp.bfloat16).reshape(wide_size, capacity * columns * channels)
    labels = jnp.sum(jnp.where(placing, places[None, :] + 1, 0), axis=1) - 1
    labels = labels.reshape(wide_size, capacity).astype(jnp.bfloat16)
    label_block = 128
    pieces = weight_pieces(w_first, w_second, band_count)
    tagged = jnp.concatenate(
        [
            outgoing,
            jnp.repeat(labels, label_block // capacity, axis=1),
            jnp.broadcast_to(pieces[None], (wide_size, pieces.shape[0])),
        ],
        axis=1,
    )
    tagged = lax.all_to_all(tagged, "wide", split_axis=0, concat_axis=0, tiled=True)
    payload = capacity * columns * channels
    arrived = tagged[:, :payload].reshape(slot_count, columns * channels)
    arrived_places = tagged[:, payload : payload + label_block : label_block // capacity]
    arrived_places = arrived_places.astype(jnp.int32).reshape(slot_count)
    kernel_first, kernel_second = assemble_weights(
        tagged[:, payload + label_block :], band_count, rows_local, channels
    )
    settle = arrived_places[None, :] == jnp.arange(slab_count, dtype=jnp.int32)[:, None]
    tile = jnp.dot(settle.astype(jnp.bfloat16), arrived, preferred_element_type=jnp.float32)
    tile = tile.astype(jnp.bfloat16).reshape(frames, band_rows, columns, channels)
    tile_wide = tile.astype(jnp.float32)
    first = jax.nn.silu(tile_wide).astype(jnp.bfloat16)
    first_ext = with_halo(first, (("rows", 1),), 1)
    act = conv_forward_t(first_ext, kernel_first).astype(jnp.bfloat16)
    second = jax.nn.silu(act.astype(jnp.float32)).astype(jnp.bfloat16)
    second_ext = with_halo(second, (("rows", 1),), 1)
    block_out = (tile_wide + conv_forward_t(second_ext, kernel_second)).astype(jnp.bfloat16)
    live = (jnp.arange(frames, dtype=jnp.int32) < lengths[0])[:, None, None, None]
    out_grad = jnp.where(live, cot[0], jnp.zeros_like(cot[0]))
    out_grad_ext = with_halo(out_grad, (("rows", 1),), 1)
    weight_second = conv_weight_grad_t(second_ext, out_grad)
    hidden_grad = conv_data_grad_t(out_grad_ext, kernel_second)
    act_grad = (hidden_grad * silu_slope(act.astype(jnp.float32))).astype(jnp.bfloat16)
    act_grad_ext = with_halo(act_grad, (("rows", 1),), 1)
    weight_first = conv_weight_grad_t(first_ext, act_grad)
    first_grad = conv_data_grad_t(act_grad_ext, kernel_first)
    grad_input = (out_grad.astype(jnp.float32) + first_grad * silu_slope(tile_wide)).astype(
        jnp.bfloat16
    )
    scale = 1.0 / math.sqrt(frames * band_rows * columns * band_count * wide_size)
    grads = jnp.stack([weight_first, weight_second]) * scale
    share_first, share_second = reduce_weight_grads(grads, band_count, wide_size)
    return (block_out[None], grad_input[None], share_first, share_second)


def solution(mesh):

    return jax.shard_map(
        body,
        mesh=mesh,
        in_specs=(
            P("wide", "rows", None, None, None),
            P("wide", "rows", None),
            P("wide", "rows", None),
            P("wide"),
            P("wide", None, "rows", None, None),
            P("wide", None),
            P("wide", None),
        ),
        out_specs=(
            P("wide", None, "rows", None, None),
            P("wide", None, "rows", None, None),
            P("wide", None),
            P("wide", None),
        ),
        check_vma=False,
    )
```

```python
import functools
import math


import jax
import jax.numpy as jnp
from jax import lax
from jax.experimental import pallas as pl
from jax.experimental.pallas import tpu as pltpu
from jax.sharding import PartitionSpec as P


def with_halo(block, sides, width):
    for axis, dim in sides:
        count = lax.axis_size(axis)
        forward = [(i, i + 1) for i in range(count - 1)]
        backward = [(target, source) for source, target in forward]
        low = lax.ppermute(
            lax.slice_in_dim(block, block.shape[dim] - width, None, axis=dim), axis, forward
        )
        high = lax.ppermute(lax.slice_in_dim(block, 0, width, axis=dim), axis, backward)
        block = jnp.concatenate([low, block, high], axis=dim)
    return block


def silu_slope(values):
    sig = jax.nn.sigmoid(values)
    return sig * (1.0 + values * (1.0 - sig))


def weight_pieces(w_first, w_second, band_count):
    rows_local, channels = w_first.shape
    part = channels // band_count
    me = lax.axis_index("rows")
    both = jnp.stack([w_first, w_second])
    mine = lax.dynamic_slice_in_dim(both, me * part, part, axis=2)
    return jnp.transpose(mine, (0, 2, 1)).reshape(2 * part * rows_local)


def assemble_weights(pieces, band_count, rows_local, channels):
    count = pieces.shape[0]
    part = channels // band_count
    block = pieces.reshape(count, 2, part, rows_local)
    block = jnp.transpose(block, (1, 2, 0, 3)).reshape(2, part, count * rows_local)
    full = rows_gather(block, band_count)
    full = jnp.transpose(full, (1, 0, 2, 3)).reshape(2, channels, count * rows_local)
    return full[0], full[1]


def rows_gather(block, band_count):
    me = lax.axis_index("rows")
    core = lax.rem(me, 2)
    chip = me // 2
    chips = band_count // 2
    held = [block]
    for shift in range(1, chips):
        route = [(r, ((r // 2 + shift) % chips) * 2 + r % 2) for r in range(band_count)]
        held.append(lax.ppermute(block, "rows", route))
    order = lax.rem(chip - jnp.arange(chips, dtype=jnp.int32) + chips, chips)
    column = jnp.take(jnp.stack(held), order, axis=0)
    partner = [(r, r + 1 - 2 * (r % 2)) for r in range(band_count)]
    got = lax.ppermute(column, "rows", partner)
    full = jnp.where(core == 0, jnp.stack([column, got], axis=1), jnp.stack([got, column], axis=1))
    return full.reshape((band_count,) + block.shape)


def _wide_sum_kernel(outer, inner, x_ref, o_ref, recv1, part, recv2, send1, got1, send2, got2):
    me = lax.axis_index("wide")
    band = lax.axis_index("rows")
    my_o = me // inner
    my_i = lax.rem(me, inner)
    mesh_id = pl.DeviceIdType.MESH
    barrier = pltpu.get_barrier_semaphore()

    def greet_inner(k, carry):
        peer = my_o * inner + lax.rem(my_i + k, inner)
        pl.semaphore_signal(barrier, 1, device_id=(peer, band), device_id_type=mesh_id)
        return carry

    def greet_outer(k, carry):
        peer = lax.rem(my_o + k, outer) * inner + my_i
        pl.semaphore_signal(barrier, 1, device_id=(peer, band), device_id_type=mesh_id)
        return carry

    lax.fori_loop(1, inner, greet_inner, 0)
    lax.fori_loop(1, outer, greet_outer, 0)
    pl.semaphore_wait(barrier, inner + outer - 2)

    def first_copy(peer_i, slot):
        return pltpu.make_async_remote_copy(
            src_ref=x_ref.at[peer_i],
            dst_ref=recv1.at[slot],
            send_sem=send1.at[peer_i],
            recv_sem=got1.at[slot],
            device_id=(my_o * inner + peer_i, band),
            device_id_type=mesh_id,
        )

    def send_first(k, carry):
        first_copy(lax.rem(my_i + k, inner), my_i).start()
        return carry

    lax.fori_loop(1, inner, send_first, 0)

    def finish_first(k, total):
        first_copy(lax.rem(my_i + k, inner), my_i).wait_send()
        source = lax.rem(my_i + inner - k, inner)
        first_copy(source, source).wait_recv()
        return total + recv1[source]

    part[...] = lax.fori_loop(1, inner, finish_first, x_ref[my_i])

    def second_copy(peer_o, slot):
        return pltpu.make_async_remote_copy(
            src_ref=part.at[peer_o],
            dst_ref=recv2.at[slot],
            send_sem=send2.at[peer_o],
            recv_sem=got2.at[slot],
            device_id=(peer_o * inner + my_i, band),
            device_id_type=mesh_id,
        )

    def send_second(k, carry):
        second_copy(lax.rem(my_o + k, outer), my_o).start()
        return carry

    lax.fori_loop(1, outer, send_second, 0)

    def finish_second(k, total):
        second_copy(lax.rem(my_o + k, outer), my_o).wait_send()
        source = lax.rem(my_o + outer - k, outer)
        second_copy(source, source).wait_recv()
        return total + recv2[source]

    o_ref[...] = lax.fori_loop(1, outer, finish_second, part[my_o])


def wide_sum(pieces):
    count, tall, lanes = pieces.shape
    inner = 8 if count % 8 == 0 else 1
    outer = count // inner
    arranged = jnp.transpose(pieces.reshape(outer, inner, tall, lanes), (1, 0, 2, 3))
    return pl.pallas_call(
        functools.partial(_wide_sum_kernel, outer, inner),
        out_shape=jax.ShapeDtypeStruct((tall, lanes), pieces.dtype),
        in_specs=[pl.BlockSpec(memory_space=pltpu.VMEM)],
        out_specs=pl.BlockSpec(memory_space=pltpu.VMEM),
        scratch_shapes=[
            pltpu.VMEM((inner, outer, tall, lanes), pieces.dtype),
            pltpu.VMEM((outer, tall, lanes), pieces.dtype),
            pltpu.VMEM((outer, tall, lanes), pieces.dtype),
            pltpu.SemaphoreType.DMA((inner,)),
            pltpu.SemaphoreType.DMA((inner,)),
            pltpu.SemaphoreType.DMA((outer,)),
            pltpu.SemaphoreType.DMA((outer,)),
        ],
        compiler_params=pltpu.CompilerParams(collective_id=0, has_side_effects=True),
    )(arranged)


def rows_reduce(blocks, band_count):
    me = lax.axis_index("rows")
    core = lax.rem(me, 2)
    chip = me // 2
    chips = band_count // 2
    pairs = blocks.reshape((chips, 2) + blocks.shape[1:])
    keep = lax.dynamic_index_in_dim(pairs, core, axis=1, keepdims=False)
    give = lax.dynamic_index_in_dim(pairs, 1 - core, axis=1, keepdims=False)
    partner = [(r, r + 1 - 2 * (r % 2)) for r in range(band_count)]
    got = lax.ppermute(give, "rows", partner)
    mine = keep.astype(jnp.float32) + got.astype(jnp.float32)
    outgoing = mine.astype(jnp.bfloat16)
    total = lax.dynamic_index_in_dim(mine, chip, axis=0, keepdims=False)
    for shift in range(1, chips):
        route = [(r, ((r // 2 + shift) % chips) * 2 + r % 2) for r in range(band_count)]
        piece = lax.dynamic_index_in_dim(outgoing, lax.rem(chip + shift, chips), axis=0, keepdims=False)
        total = total + lax.ppermute(piece, "rows", route).astype(jnp.float32)
    return total


def reduce_weight_grads(grad_t, band_count, wide_size):
    _, channels, total_rows = grad_t.shape
    part = channels // band_count
    chunk = total_rows // wide_size
    blocks = grad_t.astype(jnp.bfloat16).reshape(2, band_count, part, total_rows)
    blocks = jnp.transpose(blocks, (1, 0, 2, 3))
    band_sum = rows_reduce(blocks, band_count)
    band_sum = band_sum.reshape(2, part, wide_size, chunk)
    band_sum = jnp.transpose(band_sum, (2, 0, 1, 3)).reshape(wide_size, 2 * part * chunk)
    size = band_sum.shape[1]
    lanes = 128
    tall = -(-size // (8 * lanes)) * 8
    padded = jnp.pad(band_sum, ((0, 0), (0, tall * lanes - size)))
    share = wide_sum(padded.reshape(wide_size, tall, lanes)).reshape(1, tall * lanes)[:, :size]
    joined = rows_gather(share[0], band_count)
    joined = joined.reshape(band_count, 2, part, chunk)
    joined = jnp.transpose(joined, (1, 3, 0, 2)).reshape(2, chunk, channels)
    return joined[0], joined[1]


def conv_forward_t(extended, kernel_t):
    cout = kernel_t.shape[0]
    kernel = kernel_t.reshape(cout, 3, 3, 3, -1)
    padded = jnp.concatenate([extended[:1], extended[:1], extended], axis=0)
    result = lax.conv_general_dilated(
        padded[None], kernel, (1, 1, 1), ((0, 0), (0, 0), (1, 1)),
        dimension_numbers=("NDHWC", "ODHWI", "NDHWC"), preferred_element_type=jnp.float32,
    )
    return result[0]


def conv_weight_grad_t(extended, upstream):
    padded = jnp.concatenate([extended[:1], extended[:1], extended], axis=0)
    result = lax.conv_general_dilated(
        padded[None], upstream[None], (1, 1, 1), ((0, 0), (0, 0), (1, 1)),
        dimension_numbers=("CDHWN", "IDHWO", "CDHWN"), preferred_element_type=jnp.float32,
    )
    return result.reshape(upstream.shape[-1], -1)


def conv_data_grad_t(upstream_ext, kernel_t):
    cout = kernel_t.shape[0]
    kernel = kernel_t.reshape(cout, 3, 3, 3, -1)[:, ::-1, ::-1, ::-1, :]
    padded = jnp.pad(upstream_ext, ((2, 2), (0, 0), (0, 0), (0, 0)))
    result = lax.conv_general_dilated(
        padded[None], kernel, (1, 1, 1), ((0, 0), (0, 0), (1, 1)),
        dimension_numbers=("NDHWC", "IDHWO", "NDHWC"), preferred_element_type=jnp.float32,
    )[0]
    head = (result[0] + result[1] + result[2])[None]
    return jnp.concatenate([head, result[3:]], axis=0)


def body(slabs, dest, pos, lengths, cot, w_first, w_second):
    wide_size = lax.axis_size("wide")
    band_count = lax.axis_size("rows")
    slab_count = slabs.shape[2]
    columns = slabs.shape[3]
    channels = slabs.shape[4]
    frames = cot.shape[1]
    band_rows = cot.shape[2]
    rows_local = w_first.shape[0]
    capacity = -(-slab_count // wide_size)
    slot_count = wide_size * capacity
    targets = dest[0, 0]
    places = pos[0, 0]
    ranking = jnp.arange(slab_count, dtype=jnp.int32)
    earlier = (targets[None, :] == targets[:, None]) & (ranking[None, :] < ranking[:, None])
    slab_rank = jnp.sum(earlier.astype(jnp.int32), axis=1)
    slot_of = targets * capacity + slab_rank
    placing = slot_of[None, :] == jnp.arange(slot_count, dtype=jnp.int32)[:, None]
    flat_slabs = slabs[0, 0].reshape(slab_count, columns * channels)
    outgoing = jnp.dot(placing.astype(jnp.bfloat16), flat_slabs, preferred_element_type=jnp.float32)
    outgoing = outgoing.astype(jnp.bfloat16).reshape(wide_size, capacity * columns * channels)
    labels = jnp.sum(jnp.where(placing, places[None, :] + 1, 0), axis=1) - 1
    labels = labels.reshape(wide_size, capacity).astype(jnp.bfloat16)
    label_block = 128
    pieces = weight_pieces(w_first, w_second, band_count)
    tagged = jnp.concatenate(
        [
            outgoing,
            jnp.repeat(labels, label_block // capacity, axis=1),
            jnp.broadcast_to(pieces[None], (wide_size, pieces.shape[0])),
        ],
        axis=1,
    )
    tagged = lax.all_to_all(tagged, "wide", split_axis=0, concat_axis=0, tiled=True)
    payload = capacity * columns * channels
    arrived = tagged[:, :payload].reshape(slot_count, columns * channels)
    arrived_places = tagged[:, payload : payload + label_block : label_block // capacity]
    arrived_places = arrived_places.astype(jnp.int32).reshape(slot_count)
    kernel_first, kernel_second = assemble_weights(
        tagged[:, payload + label_block :], band_count, rows_local, channels
    )
    settle = arrived_places[None, :] == jnp.arange(slab_count, dtype=jnp.int32)[:, None]
    tile = jnp.dot(settle.astype(jnp.bfloat16), arrived, preferred_element_type=jnp.float32)
    tile = tile.astype(jnp.bfloat16).reshape(frames, band_rows, columns, channels)
    tile_wide = tile.astype(jnp.float32)
    first = jax.nn.silu(tile_wide).astype(jnp.bfloat16)
    first_ext = with_halo(first, (("rows", 1),), 1)
    act = conv_forward_t(first_ext, kernel_first).astype(jnp.bfloat16)
    second = jax.nn.silu(act.astype(jnp.float32)).astype(jnp.bfloat16)
    second_ext = with_halo(second, (("rows", 1),), 1)
    block_out = (tile_wide + conv_forward_t(second_ext, kernel_second)).astype(jnp.bfloat16)
    live = (jnp.arange(frames, dtype=jnp.int32) < lengths[0])[:, None, None, None]
    out_grad = jnp.where(live, cot[0], jnp.zeros_like(cot[0]))
    out_grad_ext = with_halo(out_grad, (("rows", 1),), 1)
    weight_second = conv_weight_grad_t(second_ext, out_grad)
    hidden_grad = conv_data_grad_t(out_grad_ext, kernel_second)
    act_grad = (hidden_grad * silu_slope(act.astype(jnp.float32))).astype(jnp.bfloat16)
    act_grad_ext = with_halo(act_grad, (("rows", 1),), 1)
    weight_first = conv_weight_grad_t(first_ext, act_grad)
    first_grad = conv_data_grad_t(act_grad_ext, kernel_first)
    grad_input = (out_grad.astype(jnp.float32) + first_grad * silu_slope(tile_wide)).astype(
        jnp.bfloat16
    )
    scale = 1.0 / math.sqrt(frames * band_rows * columns * band_count * wide_size)
    grads = jnp.stack([weight_first, weight_second]) * scale
    share_first, share_second = reduce_weight_grads(grads, band_count, wide_size)
    return (block_out[None], grad_input[None], share_first, share_second)


def solution(mesh):

    return jax.shard_map(
        body,
        mesh=mesh,
        in_specs=(
            P("wide", "rows", None, None, None),
            P("wide", "rows", None),
            P("wide", "rows", None),
            P("wide"),
            P("wide", None, "rows", None, None),
            P("wide", None),
            P("wide", None),
        ),
        out_specs=(
            P("wide", None, "rows", None, None),
            P("wide", None, "rows", None, None),
            P("wide", None),
            P("wide", None),
        ),
        check_vma=False,
    )
```

```python
import functools
import math


import jax
import jax.numpy as jnp
from jax import lax
from jax.experimental import pallas as pl
from jax.experimental.pallas import tpu as pltpu
from jax.sharding import PartitionSpec as P


def with_halo(block, sides, width):
    for axis, dim in sides:
        count = lax.axis_size(axis)
        forward = [(i, i + 1) for i in range(count - 1)]
        backward = [(target, source) for source, target in forward]
        low = lax.ppermute(
            lax.slice_in_dim(block, block.shape[dim] - width, None, axis=dim), axis, forward
        )
        high = lax.ppermute(lax.slice_in_dim(block, 0, width, axis=dim), axis, backward)
        block = jnp.concatenate([low, block, high], axis=dim)
    return block


def silu_slope(values):
    sig = jax.nn.sigmoid(values)
    return sig * (1.0 + values * (1.0 - sig))


def weight_pieces(w_first, w_second, band_count):
    rows_local, channels = w_first.shape
    part = channels // band_count
    me = lax.axis_index("rows")
    both = jnp.stack([w_first, w_second])
    mine = lax.dynamic_slice_in_dim(both, me * part, part, axis=2)
    return jnp.transpose(mine, (0, 2, 1)).reshape(2 * part * rows_local)


def assemble_weights(pieces, band_count, rows_local, channels):
    count = pieces.shape[0]
    part = channels // band_count
    block = pieces.reshape(count, 2, part, rows_local)
    block = jnp.transpose(block, (1, 2, 0, 3)).reshape(2, part, count * rows_local)
    full = rows_gather(block, band_count)
    full = jnp.transpose(full, (1, 0, 2, 3)).reshape(2, channels, count * rows_local)
    return full[0], full[1]


def rows_gather(block, band_count):
    me = lax.axis_index("rows")
    core = lax.rem(me, 2)
    chip = me // 2
    chips = band_count // 2
    held = [block]
    for shift in range(1, chips):
        route = [(r, ((r // 2 + shift) % chips) * 2 + r % 2) for r in range(band_count)]
        held.append(lax.ppermute(block, "rows", route))
    order = lax.rem(chip - jnp.arange(chips, dtype=jnp.int32) + chips, chips)
    column = jnp.take(jnp.stack(held), order, axis=0)
    partner = [(r, r + 1 - 2 * (r % 2)) for r in range(band_count)]
    got = lax.ppermute(column, "rows", partner)
    full = jnp.where(core == 0, jnp.stack([column, got], axis=1), jnp.stack([got, column], axis=1))
    return full.reshape((band_count,) + block.shape)


def _wide_sum_kernel(outer, inner, x_ref, o_ref, recv1, part, recv2, send1, got1, send2, got2):
    me = lax.axis_index("wide")
    band = lax.axis_index("rows")
    my_o = me // inner
    my_i = lax.rem(me, inner)
    mesh_id = pl.DeviceIdType.MESH
    barrier = pltpu.get_barrier_semaphore()

    def greet_inner(k, carry):
        peer = my_o * inner + lax.rem(my_i + k, inner)
        pl.semaphore_signal(barrier, 1, device_id=(peer, band), device_id_type=mesh_id)
        return carry

    def greet_outer(k, carry):
        peer = lax.rem(my_o + k, outer) * inner + my_i
        pl.semaphore_signal(barrier, 1, device_id=(peer, band), device_id_type=mesh_id)
        return carry

    lax.fori_loop(1, inner, greet_inner, 0)
    lax.fori_loop(1, outer, greet_outer, 0)
    pl.semaphore_wait(barrier, inner + outer - 2)

    def first_copy(peer_i, slot):
        return pltpu.make_async_remote_copy(
            src_ref=x_ref.at[peer_i],
            dst_ref=recv1.at[slot],
            send_sem=send1.at[peer_i],
            recv_sem=got1.at[slot],
            device_id=(my_o * inner + peer_i, band),
            device_id_type=mesh_id,
        )

    def send_first(k, carry):
        first_copy(lax.rem(my_i + k, inner), my_i).start()
        return carry

    lax.fori_loop(1, inner, send_first, 0)

    def finish_first(k, total):
        first_copy(lax.rem(my_i + k, inner), my_i).wait_send()
        source = lax.rem(my_i + inner - k, inner)
        first_copy(source, source).wait_recv()
        return total + recv1[source]

    part[...] = lax.fori_loop(1, inner, finish_first, x_ref[my_i])

    def second_copy(peer_o, slot):
        return pltpu.make_async_remote_copy(
            src_ref=part.at[peer_o],
            dst_ref=recv2.at[slot],
            send_sem=send2.at[peer_o],
            recv_sem=got2.at[slot],
            device_id=(peer_o * inner + my_i, band),
            device_id_type=mesh_id,
        )

    def send_second(k, carry):
        second_copy(lax.rem(my_o + k, outer), my_o).start()
        return carry

    lax.fori_loop(1, outer, send_second, 0)

    def finish_second(k, total):
        second_copy(lax.rem(my_o + k, outer), my_o).wait_send()
        source = lax.rem(my_o + outer - k, outer)
        second_copy(source, source).wait_recv()
        return total + recv2[source]

    o_ref[...] = lax.fori_loop(1, outer, finish_second, part[my_o])


def wide_sum(pieces):
    count, tall, lanes = pieces.shape
    inner = 8 if count % 8 == 0 else 1
    outer = count // inner
    arranged = jnp.transpose(pieces.reshape(outer, inner, tall, lanes), (1, 0, 2, 3))
    return pl.pallas_call(
        functools.partial(_wide_sum_kernel, outer, inner),
        out_shape=jax.ShapeDtypeStruct((tall, lanes), pieces.dtype),
        in_specs=[pl.BlockSpec(memory_space=pltpu.VMEM)],
        out_specs=pl.BlockSpec(memory_space=pltpu.VMEM),
        scratch_shapes=[
            pltpu.VMEM((inner, outer, tall, lanes), pieces.dtype),
            pltpu.VMEM((outer, tall, lanes), pieces.dtype),
            pltpu.VMEM((outer, tall, lanes), pieces.dtype),
            pltpu.SemaphoreType.DMA((inner,)),
            pltpu.SemaphoreType.DMA((inner,)),
            pltpu.SemaphoreType.DMA((outer,)),
            pltpu.SemaphoreType.DMA((outer,)),
        ],
        compiler_params=pltpu.CompilerParams(collective_id=0, has_side_effects=True),
    )(arranged)


def rows_reduce(blocks, band_count):
    me = lax.axis_index("rows")
    core = lax.rem(me, 2)
    chip = me // 2
    chips = band_count // 2
    pairs = blocks.reshape((chips, 2) + blocks.shape[1:])
    keep = lax.dynamic_index_in_dim(pairs, core, axis=1, keepdims=False)
    give = lax.dynamic_index_in_dim(pairs, 1 - core, axis=1, keepdims=False)
    partner = [(r, r + 1 - 2 * (r % 2)) for r in range(band_count)]
    got = lax.ppermute(give, "rows", partner)
    mine = keep.astype(jnp.float32) + got.astype(jnp.float32)
    outgoing = mine.astype(jnp.bfloat16)
    total = lax.dynamic_index_in_dim(mine, chip, axis=0, keepdims=False)
    for shift in range(1, chips):
        route = [(r, ((r // 2 + shift) % chips) * 2 + r % 2) for r in range(band_count)]
        piece = lax.dynamic_index_in_dim(outgoing, lax.rem(chip + shift, chips), axis=0, keepdims=False)
        total = total + lax.ppermute(piece, "rows", route).astype(jnp.float32)
    return total


def reduce_weight_grads(grad_t, band_count, wide_size):
    _, channels, total_rows = grad_t.shape
    part = channels // band_count
    chunk = total_rows // wide_size
    blocks = grad_t.reshape(2, band_count, part, total_rows)
    blocks = jnp.transpose(blocks, (1, 0, 2, 3))
    band_sum = rows_reduce(blocks, band_count)
    band_sum = band_sum.reshape(2, part, wide_size, chunk)
    band_sum = jnp.transpose(band_sum, (2, 0, 1, 3)).reshape(wide_size, 2 * part * chunk)
    size = band_sum.shape[1]
    lanes = 128
    tall = -(-size // (8 * lanes)) * 8
    padded = jnp.pad(band_sum, ((0, 0), (0, tall * lanes - size)))
    share = wide_sum(padded.reshape(wide_size, tall, lanes)).reshape(1, tall * lanes)[:, :size]
    joined = lax.all_to_all(
        jnp.broadcast_to(share, (band_count,) + share.shape[1:]), "rows", 0, 0, tiled=True
    )
    joined = joined.reshape(band_count, 2, part, chunk)
    joined = jnp.transpose(joined, (1, 3, 0, 2)).reshape(2, chunk, channels)
    return joined[0], joined[1]


def conv_forward_t(extended, kernel_t):
    cout = kernel_t.shape[0]
    kernel = kernel_t.reshape(cout, 3, 3, 3, -1)
    padded = jnp.concatenate([extended[:1], extended[:1], extended], axis=0)
    result = lax.conv_general_dilated(
        padded[None], kernel, (1, 1, 1), ((0, 0), (0, 0), (1, 1)),
        dimension_numbers=("NDHWC", "ODHWI", "NDHWC"), preferred_element_type=jnp.float32,
    )
    return result[0]


def conv_weight_grad_t(extended, upstream):
    padded = jnp.concatenate([extended[:1], extended[:1], extended], axis=0)
    result = lax.conv_general_dilated(
        padded[None], upstream[None], (1, 1, 1), ((0, 0), (0, 0), (1, 1)),
        dimension_numbers=("CDHWN", "IDHWO", "CDHWN"), preferred_element_type=jnp.float32,
    )
    return result.reshape(upstream.shape[-1], -1)


def conv_data_grad_t(upstream_ext, kernel_t):
    cout = kernel_t.shape[0]
    kernel = kernel_t.reshape(cout, 3, 3, 3, -1)[:, ::-1, ::-1, ::-1, :]
    padded = jnp.pad(upstream_ext, ((2, 2), (0, 0), (0, 0), (0, 0)))
    result = lax.conv_general_dilated(
        padded[None], kernel, (1, 1, 1), ((0, 0), (0, 0), (1, 1)),
        dimension_numbers=("NDHWC", "IDHWO", "NDHWC"), preferred_element_type=jnp.float32,
    )[0]
    head = (result[0] + result[1] + result[2])[None]
    return jnp.concatenate([head, result[3:]], axis=0)


def body(slabs, dest, pos, lengths, cot, w_first, w_second):
    wide_size = lax.axis_size("wide")
    band_count = lax.axis_size("rows")
    slab_count = slabs.shape[2]
    columns = slabs.shape[3]
    channels = slabs.shape[4]
    frames = cot.shape[1]
    band_rows = cot.shape[2]
    rows_local = w_first.shape[0]
    capacity = -(-slab_count // wide_size)
    slot_count = wide_size * capacity
    targets = dest[0, 0]
    places = pos[0, 0]
    ranking = jnp.arange(slab_count, dtype=jnp.int32)
    earlier = (targets[None, :] == targets[:, None]) & (ranking[None, :] < ranking[:, None])
    slab_rank = jnp.sum(earlier.astype(jnp.int32), axis=1)
    slot_of = targets * capacity + slab_rank
    placing = slot_of[None, :] == jnp.arange(slot_count, dtype=jnp.int32)[:, None]
    flat_slabs = slabs[0, 0].reshape(slab_count, columns * channels)
    outgoing = jnp.dot(placing.astype(jnp.bfloat16), flat_slabs, preferred_element_type=jnp.float32)
    outgoing = outgoing.astype(jnp.bfloat16).reshape(wide_size, capacity * columns * channels)
    labels = jnp.sum(jnp.where(placing, places[None, :] + 1, 0), axis=1) - 1
    labels = labels.reshape(wide_size, capacity).astype(jnp.bfloat16)
    label_block = 128
    pieces = weight_pieces(w_first, w_second, band_count)
    tagged = jnp.concatenate(
        [
            outgoing,
            jnp.repeat(labels, label_block // capacity, axis=1),
            jnp.broadcast_to(pieces[None], (wide_size, pieces.shape[0])),
        ],
        axis=1,
    )
    tagged = lax.all_to_all(tagged, "wide", split_axis=0, concat_axis=0, tiled=True)
    payload = capacity * columns * channels
    arrived = tagged[:, :payload].reshape(slot_count, columns * channels)
    arrived_places = tagged[:, payload : payload + label_block : label_block // capacity]
    arrived_places = arrived_places.astype(jnp.int32).reshape(slot_count)
    kernel_first, kernel_second = assemble_weights(
        tagged[:, payload + label_block :], band_count, rows_local, channels
    )
    settle = arrived_places[None, :] == jnp.arange(slab_count, dtype=jnp.int32)[:, None]
    tile = jnp.dot(settle.astype(jnp.bfloat16), arrived, preferred_element_type=jnp.float32)
    tile = tile.astype(jnp.bfloat16).reshape(frames, band_rows, columns, channels)
    tile_wide = tile.astype(jnp.float32)
    first = jax.nn.silu(tile_wide).astype(jnp.bfloat16)
    first_ext = with_halo(first, (("rows", 1),), 1)
    act = conv_forward_t(first_ext, kernel_first).astype(jnp.bfloat16)
    second = jax.nn.silu(act.astype(jnp.float32)).astype(jnp.bfloat16)
    second_ext = with_halo(second, (("rows", 1),), 1)
    block_out = (tile_wide + conv_forward_t(second_ext, kernel_second)).astype(jnp.bfloat16)
    live = (jnp.arange(frames, dtype=jnp.int32) < lengths[0])[:, None, None, None]
    out_grad = jnp.where(live, cot[0], jnp.zeros_like(cot[0]))
    out_grad_ext = with_halo(out_grad, (("rows", 1),), 1)
    weight_second = conv_weight_grad_t(second_ext, out_grad)
    hidden_grad = conv_data_grad_t(out_grad_ext, kernel_second)
    act_grad = (hidden_grad * silu_slope(act.astype(jnp.float32))).astype(jnp.bfloat16)
    act_grad_ext = with_halo(act_grad, (("rows", 1),), 1)
    weight_first = conv_weight_grad_t(first_ext, act_grad)
    first_grad = conv_data_grad_t(act_grad_ext, kernel_first)
    grad_input = (out_grad.astype(jnp.float32) + first_grad * silu_slope(tile_wide)).astype(
        jnp.bfloat16
    )
    scale = 1.0 / math.sqrt(frames * band_rows * columns * band_count * wide_size)
    grads = jnp.stack(
        [(weight_first * scale).astype(jnp.bfloat16), (weight_second * scale).astype(jnp.bfloat16)]
    )
    share_first, share_second = reduce_weight_grads(grads, band_count, wide_size)
    return (block_out[None], grad_input[None], share_first, share_second)


def solution(mesh):

    return jax.shard_map(
        body,
        mesh=mesh,
        in_specs=(
            P("wide", "rows", None, None, None),
            P("wide", "rows", None),
            P("wide", "rows", None),
            P("wide"),
            P("wide", None, "rows", None, None),
            P("wide", None),
            P("wide", None),
        ),
        out_specs=(
            P("wide", None, "rows", None, None),
            P("wide", None, "rows", None, None),
            P("wide", None),
            P("wide", None),
        ),
        check_vma=False,
    )
```

```python
import functools
import math


import jax
import jax.numpy as jnp
from jax import lax
from jax.experimental import pallas as pl
from jax.experimental.pallas import tpu as pltpu
from jax.sharding import PartitionSpec as P


def with_halo(block, sides, width):
    for axis, dim in sides:
        count = lax.axis_size(axis)
        forward = [(i, i + 1) for i in range(count - 1)]
        backward = [(target, source) for source, target in forward]
        low = lax.ppermute(
            lax.slice_in_dim(block, block.shape[dim] - width, None, axis=dim), axis, forward
        )
        high = lax.ppermute(lax.slice_in_dim(block, 0, width, axis=dim), axis, backward)
        block = jnp.concatenate([low, block, high], axis=dim)
    return block


def silu_slope(values):
    sig = jax.nn.sigmoid(values)
    return sig * (1.0 + values * (1.0 - sig))


def weight_pieces(w_first, w_second, band_count):
    rows_local, channels = w_first.shape
    part = channels // band_count
    me = lax.axis_index("rows")
    both = jnp.stack([w_first, w_second])
    mine = lax.dynamic_slice_in_dim(both, me * part, part, axis=2)
    return jnp.transpose(mine, (0, 2, 1)).reshape(2 * part * rows_local)


def assemble_weights(pieces, band_count, rows_local, channels):
    count = pieces.shape[0]
    part = channels // band_count
    block = pieces.reshape(count, 2, part, rows_local)
    block = jnp.transpose(block, (1, 2, 0, 3)).reshape(2, part, count * rows_local)
    full = rows_gather(block, band_count)
    full = jnp.transpose(full, (1, 0, 2, 3)).reshape(2, channels, count * rows_local)
    return full[0], full[1]


def rows_gather(block, band_count):
    me = lax.axis_index("rows")
    core = lax.rem(me, 2)
    chip = me // 2
    chips = band_count // 2
    held = [block]
    for shift in range(1, chips):
        route = [(r, ((r // 2 + shift) % chips) * 2 + r % 2) for r in range(band_count)]
        held.append(lax.ppermute(block, "rows", route))
    order = lax.rem(chip - jnp.arange(chips, dtype=jnp.int32) + chips, chips)
    column = jnp.take(jnp.stack(held), order, axis=0)
    partner = [(r, r + 1 - 2 * (r % 2)) for r in range(band_count)]
    got = lax.ppermute(column, "rows", partner)
    full = jnp.where(core == 0, jnp.stack([column, got], axis=1), jnp.stack([got, column], axis=1))
    return full.reshape((band_count,) + block.shape)


def _wide_sum_kernel(outer, inner, x_ref, o_ref, recv1, part, recv2, send1, got1, send2, got2):
    me = lax.axis_index("wide")
    band = lax.axis_index("rows")
    my_o = me // inner
    my_i = lax.rem(me, inner)
    mesh_id = pl.DeviceIdType.MESH
    barrier = pltpu.get_barrier_semaphore()

    def greet_inner(k, carry):
        peer = my_o * inner + lax.rem(my_i + k, inner)
        pl.semaphore_signal(barrier, 1, device_id=(peer, band), device_id_type=mesh_id)
        return carry

    def greet_outer(k, carry):
        peer = lax.rem(my_o + k, outer) * inner + my_i
        pl.semaphore_signal(barrier, 1, device_id=(peer, band), device_id_type=mesh_id)
        return carry

    lax.fori_loop(1, inner, greet_inner, 0)
    lax.fori_loop(1, outer, greet_outer, 0)
    pl.semaphore_wait(barrier, inner + outer - 2)

    def first_copy(peer_i, slot):
        return pltpu.make_async_remote_copy(
            src_ref=x_ref.at[peer_i],
            dst_ref=recv1.at[slot],
            send_sem=send1.at[peer_i],
            recv_sem=got1.at[slot],
            device_id=(my_o * inner + peer_i, band),
            device_id_type=mesh_id,
        )

    def send_first(k, carry):
        first_copy(lax.rem(my_i + k, inner), my_i).start()
        return carry

    lax.fori_loop(1, inner, send_first, 0)

    def finish_first(k, total):
        first_copy(lax.rem(my_i + k, inner), my_i).wait_send()
        source = lax.rem(my_i + inner - k, inner)
        first_copy(source, source).wait_recv()
        return total + recv1[source].astype(jnp.float32)

    part[...] = lax.fori_loop(1, inner, finish_first, x_ref[my_i].astype(jnp.float32))

    def second_copy(peer_o, slot):
        return pltpu.make_async_remote_copy(
            src_ref=part.at[peer_o],
            dst_ref=recv2.at[slot],
            send_sem=send2.at[peer_o],
            recv_sem=got2.at[slot],
            device_id=(peer_o * inner + my_i, band),
            device_id_type=mesh_id,
        )

    def send_second(k, carry):
        second_copy(lax.rem(my_o + k, outer), my_o).start()
        return carry

    lax.fori_loop(1, outer, send_second, 0)

    def finish_second(k, total):
        second_copy(lax.rem(my_o + k, outer), my_o).wait_send()
        source = lax.rem(my_o + outer - k, outer)
        second_copy(source, source).wait_recv()
        return total + recv2[source]

    o_ref[...] = lax.fori_loop(1, outer, finish_second, part[my_o])


def wide_sum(pieces):
    count, tall, lanes = pieces.shape
    inner = 8 if count % 8 == 0 else 1
    outer = count // inner
    arranged = jnp.transpose(pieces.reshape(outer, inner, tall, lanes), (1, 0, 2, 3))
    return pl.pallas_call(
        functools.partial(_wide_sum_kernel, outer, inner),
        out_shape=jax.ShapeDtypeStruct((tall, lanes), jnp.float32),
        in_specs=[pl.BlockSpec(memory_space=pltpu.VMEM)],
        out_specs=pl.BlockSpec(memory_space=pltpu.VMEM),
        scratch_shapes=[
            pltpu.VMEM((inner, outer, tall, lanes), pieces.dtype),
            pltpu.VMEM((outer, tall, lanes), jnp.float32),
            pltpu.VMEM((outer, tall, lanes), jnp.float32),
            pltpu.SemaphoreType.DMA((inner,)),
            pltpu.SemaphoreType.DMA((inner,)),
            pltpu.SemaphoreType.DMA((outer,)),
            pltpu.SemaphoreType.DMA((outer,)),
        ],
        compiler_params=pltpu.CompilerParams(collective_id=0, has_side_effects=True),
    )(arranged)


def rows_reduce(blocks, band_count):
    me = lax.axis_index("rows")
    core = lax.rem(me, 2)
    chip = me // 2
    chips = band_count // 2
    pairs = blocks.reshape((chips, 2) + blocks.shape[1:])
    keep = lax.dynamic_index_in_dim(pairs, core, axis=1, keepdims=False)
    give = lax.dynamic_index_in_dim(pairs, 1 - core, axis=1, keepdims=False)
    partner = [(r, r + 1 - 2 * (r % 2)) for r in range(band_count)]
    got = lax.ppermute(give, "rows", partner)
    mine = keep.astype(jnp.float32) + got.astype(jnp.float32)
    outgoing = mine.astype(jnp.bfloat16)
    total = lax.dynamic_index_in_dim(mine, chip, axis=0, keepdims=False)
    for shift in range(1, chips):
        route = [(r, ((r // 2 + shift) % chips) * 2 + r % 2) for r in range(band_count)]
        piece = lax.dynamic_index_in_dim(outgoing, lax.rem(chip + shift, chips), axis=0, keepdims=False)
        total = total + lax.ppermute(piece, "rows", route).astype(jnp.float32)
    return total


def reduce_weight_grads(grad_t, band_count, wide_size):
    _, channels, total_rows = grad_t.shape
    part = channels // band_count
    chunk = total_rows // wide_size
    blocks = grad_t.reshape(2, band_count, part, total_rows)
    blocks = jnp.transpose(blocks, (1, 0, 2, 3))
    band_sum = rows_reduce(blocks, band_count)
    band_sum = band_sum.reshape(2, part, wide_size, chunk)
    band_sum = jnp.transpose(band_sum, (2, 0, 1, 3)).reshape(wide_size, 2 * part * chunk)
    size = band_sum.shape[1]
    lanes = 128
    tall = -(-size // (8 * lanes)) * 8
    padded = jnp.pad(band_sum, ((0, 0), (0, tall * lanes - size)))
    share = wide_sum(padded.reshape(wide_size, tall, lanes).astype(jnp.bfloat16)).reshape(1, tall * lanes)[:, :size]
    joined = lax.all_to_all(
        jnp.broadcast_to(share, (band_count,) + share.shape[1:]), "rows", 0, 0, tiled=True
    )
    joined = joined.reshape(band_count, 2, part, chunk)
    joined = jnp.transpose(joined, (1, 3, 0, 2)).reshape(2, chunk, channels)
    return joined[0], joined[1]


def conv_forward_t(extended, kernel_t):
    cout = kernel_t.shape[0]
    kernel = kernel_t.reshape(cout, 3, 3, 3, -1)
    padded = jnp.concatenate([extended[:1], extended[:1], extended], axis=0)
    result = lax.conv_general_dilated(
        padded[None], kernel, (1, 1, 1), ((0, 0), (0, 0), (1, 1)),
        dimension_numbers=("NDHWC", "ODHWI", "NDHWC"), preferred_element_type=jnp.float32,
    )
    return result[0]


def conv_weight_grad_t(extended, upstream):
    padded = jnp.concatenate([extended[:1], extended[:1], extended], axis=0)
    result = lax.conv_general_dilated(
        padded[None], upstream[None], (1, 1, 1), ((0, 0), (0, 0), (1, 1)),
        dimension_numbers=("CDHWN", "IDHWO", "CDHWN"), preferred_element_type=jnp.float32,
    )
    return result.reshape(upstream.shape[-1], -1)


def conv_data_grad_t(upstream_ext, kernel_t):
    cout = kernel_t.shape[0]
    kernel = kernel_t.reshape(cout, 3, 3, 3, -1)[:, ::-1, ::-1, ::-1, :]
    padded = jnp.pad(upstream_ext, ((2, 2), (0, 0), (0, 0), (0, 0)))
    result = lax.conv_general_dilated(
        padded[None], kernel, (1, 1, 1), ((0, 0), (0, 0), (1, 1)),
        dimension_numbers=("NDHWC", "IDHWO", "NDHWC"), preferred_element_type=jnp.float32,
    )[0]
    head = (result[0] + result[1] + result[2])[None]
    return jnp.concatenate([head, result[3:]], axis=0)


def body(slabs, dest, pos, lengths, cot, w_first, w_second):
    wide_size = lax.axis_size("wide")
    band_count = lax.axis_size("rows")
    slab_count = slabs.shape[2]
    columns = slabs.shape[3]
    channels = slabs.shape[4]
    frames = cot.shape[1]
    band_rows = cot.shape[2]
    rows_local = w_first.shape[0]
    capacity = -(-slab_count // wide_size)
    slot_count = wide_size * capacity
    targets = dest[0, 0]
    places = pos[0, 0]
    ranking = jnp.arange(slab_count, dtype=jnp.int32)
    earlier = (targets[None, :] == targets[:, None]) & (ranking[None, :] < ranking[:, None])
    slab_rank = jnp.sum(earlier.astype(jnp.int32), axis=1)
    slot_of = targets * capacity + slab_rank
    placing = slot_of[None, :] == jnp.arange(slot_count, dtype=jnp.int32)[:, None]
    flat_slabs = slabs[0, 0].reshape(slab_count, columns * channels)
    outgoing = jnp.dot(placing.astype(jnp.bfloat16), flat_slabs, preferred_element_type=jnp.float32)
    outgoing = outgoing.astype(jnp.bfloat16).reshape(wide_size, capacity * columns * channels)
    labels = jnp.sum(jnp.where(placing, places[None, :] + 1, 0), axis=1) - 1
    labels = labels.reshape(wide_size, capacity).astype(jnp.bfloat16)
    label_block = 128
    pieces = weight_pieces(w_first, w_second, band_count)
    tagged = jnp.concatenate(
        [
            outgoing,
            jnp.repeat(labels, label_block // capacity, axis=1),
            jnp.broadcast_to(pieces[None], (wide_size, pieces.shape[0])),
        ],
        axis=1,
    )
    tagged = lax.all_to_all(tagged, "wide", split_axis=0, concat_axis=0, tiled=True)
    payload = capacity * columns * channels
    arrived = tagged[:, :payload].reshape(slot_count, columns * channels)
    arrived_places = tagged[:, payload : payload + label_block : label_block // capacity]
    arrived_places = arrived_places.astype(jnp.int32).reshape(slot_count)
    kernel_first, kernel_second = assemble_weights(
        tagged[:, payload + label_block :], band_count, rows_local, channels
    )
    settle = arrived_places[None, :] == jnp.arange(slab_count, dtype=jnp.int32)[:, None]
    tile = jnp.dot(settle.astype(jnp.bfloat16), arrived, preferred_element_type=jnp.float32)
    tile = tile.astype(jnp.bfloat16).reshape(frames, band_rows, columns, channels)
    tile_wide = tile.astype(jnp.float32)
    first = jax.nn.silu(tile_wide).astype(jnp.bfloat16)
    first_ext = with_halo(first, (("rows", 1),), 1)
    act = conv_forward_t(first_ext, kernel_first).astype(jnp.bfloat16)
    second = jax.nn.silu(act.astype(jnp.float32)).astype(jnp.bfloat16)
    second_ext = with_halo(second, (("rows", 1),), 1)
    block_out = (tile_wide + conv_forward_t(second_ext, kernel_second)).astype(jnp.bfloat16)
    live = (jnp.arange(frames, dtype=jnp.int32) < lengths[0])[:, None, None, None]
    out_grad = jnp.where(live, cot[0], jnp.zeros_like(cot[0]))
    out_grad_ext = with_halo(out_grad, (("rows", 1),), 1)
    weight_second = conv_weight_grad_t(second_ext, out_grad)
    hidden_grad = conv_data_grad_t(out_grad_ext, kernel_second)
    act_grad = (hidden_grad * silu_slope(act.astype(jnp.float32))).astype(jnp.bfloat16)
    act_grad_ext = with_halo(act_grad, (("rows", 1),), 1)
    weight_first = conv_weight_grad_t(first_ext, act_grad)
    first_grad = conv_data_grad_t(act_grad_ext, kernel_first)
    grad_input = (out_grad.astype(jnp.float32) + first_grad * silu_slope(tile_wide)).astype(
        jnp.bfloat16
    )
    scale = 1.0 / math.sqrt(frames * band_rows * columns * band_count * wide_size)
    grads = jnp.stack(
        [(weight_first * scale).astype(jnp.bfloat16), (weight_second * scale).astype(jnp.bfloat16)]
    )
    share_first, share_second = reduce_weight_grads(grads, band_count, wide_size)
    return (block_out[None], grad_input[None], share_first, share_second)


def solution(mesh):

    return jax.shard_map(
        body,
        mesh=mesh,
        in_specs=(
            P("wide", "rows", None, None, None),
            P("wide", "rows", None),
            P("wide", "rows", None),
            P("wide"),
            P("wide", None, "rows", None, None),
            P("wide", None),
            P("wide", None),
        ),
        out_specs=(
            P("wide", None, "rows", None, None),
            P("wide", None, "rows", None, None),
            P("wide", None),
            P("wide", None),
        ),
        check_vma=False,
    )
```
